32 devices in a mesh: comp: 4 (over y, x), cell: 8 (over z, core).
Axes of the slice: x: 2, y: 2, z: 4, core: 2. Of those that a mesh axis runs over, the one named last changes fastest.
Arguments:
- biomass: float32 [48, 64, 4096], P(None, None, ('comp', 'cell')), may hold values from 0.1 to 2
- patch_area: float32 [48, 4096], P(None, ('comp', 'cell')), may hold values from 0.005 to 0.04
- cohort_traits: float32 [4, 64], replicated, may hold values from 0.1 to 1
- cell_forcing: float32 [5, 4096], P(None, ('comp', 'cell')), may hold values from 0.1 to 1
- disturb_weight: float32 [4, 4096], P(None, ('comp', 'cell')), may hold values from 0 to 0.25
- transitions: float32 [4, 48, 48], replicated, may hold values from 0 to 1
- land_source: int32 [32768], P(('comp', 'cell')), may hold values from -1 to 127, as said below
- pair_share: float32 [32768], P(('comp', 'cell')), may hold values from 0.05 to 0.35
- river_target: int32 [32768], P(('comp', 'cell')), may hold values from -1 to 2047, as said below
- downstream_step: int32 [65536], P(('comp', 'cell')), may hold values from 0 to 2047
- river_water: float32 [4, 65536], P(None, ('comp', 'cell')), may hold values from 0.5 to 2
- river_rates: float32 [4, 65536], P(None, ('comp', 'cell')), may hold values from 0.05 to 0.8
- capacity: float32 [65536], P(('comp', 'cell')), may hold values from 0.5 to 5
Outputs:
- new_biomass: float32 [48, 64, 4096], P(None, None, ('comp', 'cell'))
- flooded: float32 [4096], P(('comp', 'cell'))
- river_state: float32 [4, 65536], P(None, ('comp', 'cell'))
The draws below stay inside these ranges and needn't reach their ends.
Inputs may be any that keep to these rules, and one draw needn't show every extreme that they name: `land_source`: A device's list has one block of 32 rows for each receiving device, in comp+cell order; live rows come first in every block, padding rows hold -1. Every device has at least one full block, and one receiving device gets full blocks from every device. `river_target`: row s of block i on device j is live exactly when row s of block j on device i of land_source is live, and then names the receiving river cell of device j; padding rows hold -1.
All inputs are finite; a program needn't handle non-finite values.
Results may differ from the reference program's by a relative error of at most 0.0001.
Values sent between devices are 32-bit elements; how exact they have to be, the bound alone decides.
No kernel may reach another device: no remote copies, remote signals or barrier semaphores. Data moves between devices by JAX's collectives and lax.ppermute only.
A program may use at most 64 MiB of HBM per device.

```python
import math
import jax
import jax.numpy as jnp
from jax import lax

P_SIZE = 48
K = 64
TYPES = 4
NSUB = 12
LC = 128
RC = 2048
SLOT = 32
LAND = 4096
RIVER = 65536
LIST = 32768
N_COMP = 4
N_CELL = 8


def coupler_lists(key):
    devices = LAND // LC
    count_key, source_key, target_key, basin_key = jax.random.split(jax.random.fold_in(key, 7), 4)
    counts = jax.random.randint(count_key, (devices, devices), SLOT // 4, SLOT + 1)
    basin = jax.random.randint(basin_key, (), 0, devices)
    sender_ids = jnp.arange(devices)[:, None]
    receiver_ids = jnp.arange(devices)[None, :]
    full_block = (receiver_ids == basin) | (receiver_ids == (sender_ids + 1) % devices)
    counts = jnp.where(full_block, SLOT, counts)
    slot_ids = jnp.arange(SLOT)[None, None, :]
    is_live = slot_ids < counts[:, :, None]
    sources = jax.random.randint(source_key, (devices, devices, SLOT), 0, LC)
    targets = jax.random.randint(target_key, (devices, devices, SLOT), 0, RC)
    first_row = (slot_ids == 0) & (receiver_ids[:, :, None] == basin)
    sources = jnp.where(first_row, LC - 1, sources)
    targets = jnp.where(first_row, RC - 1, targets)
    return (jnp.where(is_live, sources, -1), jnp.where(is_live, targets, -1))


def draw_land_source(key, part):
    sources, targets = coupler_lists(key)
    return sources.reshape(-1).astype(jnp.int32)


def draw_river_target(key, part):
    sources, targets = coupler_lists(key)
    return targets.transpose(1, 0, 2).reshape(-1).astype(jnp.int32)


def draw_downstream_step(key, part):
    jump_key, outlet_key = jax.random.split(jax.random.fold_in(key, 11))
    steps = jax.random.randint(jump_key, (RIVER,), 1, RC)
    position = jnp.arange(RIVER)
    steps = jnp.where(jax.random.randint(outlet_key, (RIVER,), 0, 32) == 0, 0, steps)
    steps = jnp.where(position % RC == 0, RC - 1, steps)
    steps = jnp.where(position + steps >= RIVER, 0, steps)
    return steps.astype(jnp.int32)


def draw_transitions(key, part):
    spread_part = jax.random.uniform(jax.random.fold_in(key, 5), (TYPES, P_SIZE, P_SIZE), jnp.float32, 0.0, 1.0 / P_SIZE)
    diagonal = (jnp.arange(P_SIZE)[:, None] == jnp.arange(P_SIZE)[None, :]).astype(jnp.float32)
    return spread_part + 0.5 * diagonal[None]


def steps_of(stream_key, extent, shards, low, high):
    def one(dim, shards_of):
        heights = jax.random.uniform(jax.random.fold_in(jax.random.fold_in(stream_key, 6), dim), (shards_of,), jnp.float32, low / len(shards), high / len(shards))
        return jnp.repeat(jnp.exp(heights), extent[dim] // shards_of).reshape((-1,) + (1,) * (len(extent) - dim - 1))

    gain = one(*shards[0])
    for cut in shards[1:]:
        gain = gain * one(*cut)
    return gain


def setup_inputs(seed: int = 0) -> dict:
    key_of = jax.random.split(jax.random.key(seed), 14)
    return {
        "biomass": jnp.clip(jnp.exp(math.log(2.0) - 2.9957323 * jax.random.uniform(key_of[0], (P_SIZE, K, LAND), jnp.float32) ** steps_of(key_of[0], (P_SIZE, K, LAND), ((2, 32),), -0.2, 0.2)), 0.1, 2.0),
        "patch_area": jnp.clip(jnp.exp(math.log(0.04) - 2.0794415 * jax.random.uniform(key_of[1], (P_SIZE, LAND), jnp.float32) ** steps_of(key_of[1], (P_SIZE, LAND), ((1, 32),), -0.2, 0.2)), 0.005, 0.04),
        "cohort_traits": jnp.clip(jax.random.uniform(key_of[2], (4, K), jnp.float32, 0.1, 1.0), 0.1, 1.0),
        "cell_forcing": jnp.clip(0.1 + 0.9 * jax.random.uniform(key_of[3], (5, LAND), jnp.float32) ** steps_of(key_of[3], (5, LAND), ((1, 32),), -0.2, 0.2), 0.1, 1.0),
        "disturb_weight": jnp.clip(0.25 * jax.random.uniform(key_of[4], (TYPES, LAND), jnp.float32) ** steps_of(key_of[4], (TYPES, LAND), ((1, 32),), -0.2, 0.2), 0.0, 0.25),
        "transitions": draw_transitions(jax.random.fold_in(key_of[13], 71), 0),
        "land_source": draw_land_source(jax.random.fold_in(key_of[13], 71), 0),
        "pair_share": jnp.clip(0.05 + 0.29999999 * jax.random.uniform(key_of[7], (LIST,), jnp.float32) ** steps_of(key_of[7], (LIST,), ((0, 32),), -0.2, 0.2), 0.05, 0.35),
        "river_target": draw_river_target(jax.random.fold_in(key_of[13], 71), 0),
        "downstream_step": draw_downstream_step(jax.random.fold_in(key_of[13], 71), 0),
        "river_water": jnp.clip(jnp.exp(math.log(2.0) - 1.3862944 * jax.random.uniform(key_of[10], (4, RIVER), jnp.float32) ** steps_of(key_of[10], (4, RIVER), ((1, 32),), -0.2, 0.2)), 0.5, 2.0),
        "river_rates": jnp.clip(jnp.exp(math.log(0.8) - 2.7725887 * jax.random.uniform(key_of[11], (4, RIVER), jnp.float32) ** steps_of(key_of[11], (4, RIVER), ((1, 32),), -0.2, 0.2)), 0.05, 0.8),
        "capacity": jnp.clip(jnp.exp(math.log(5.0) - 2.3025851 * jax.random.uniform(key_of[12], (RIVER,), jnp.float32) ** steps_of(key_of[12], (RIVER,), ((0, 32),), -0.2, 0.2)), 0.5, 5.0),
    }


highest = lax.Precision.HIGHEST


def canopy(biomass, patch_area, cohort_traits, cell_forcing):
    leaf_area = biomass * cohort_traits[0][None, :, None]
    bin_count = biomass.shape[1]
    taller_mask = (jnp.arange(bin_count)[None, :] > jnp.arange(bin_count)[:, None]).astype(jnp.float32)
    leaf_above = jnp.einsum("kj,pjc->pkc", taller_mask, leaf_area, precision=highest)
    light_level = cell_forcing[0]
    assimilation = cohort_traits[1][None, :, None] * leaf_area * jnp.exp(-0.05 * leaf_above) * (light_level / (light_level + 0.5))[None, None, :]
    transpiration = 0.5 * jnp.sum(patch_area * jnp.sum(assimilation, axis=1), axis=0)
    wet_rain = cell_forcing[1] * cell_forcing[2]
    runoff = jnp.stack([wet_rain * (1.0 - cell_forcing[4]), wet_rain * cell_forcing[4], cell_forcing[3] * jnp.exp(-0.5 * transpiration)])
    grown_mass = biomass * (1.0 - 0.1 * cohort_traits[2])[None, :, None] + 0.5 * assimilation
    return grown_mass, runoff


def transit(grown_mass, disturb_weight, transitions):
    patches, bin_count, cell_count = grown_mass.shape
    flat_mass = grown_mass.reshape(patches, bin_count * cell_count)
    transited = jnp.zeros_like(grown_mass)
    for kind_index in range(transitions.shape[0]):
        moved_mass = jnp.dot(transitions[kind_index], flat_mass, precision=highest, preferred_element_type=jnp.float32)
        transited = transited + moved_mass.reshape(patches, bin_count, cell_count) * disturb_weight[kind_index][None, None, :]
    return transited


def reference(biomass, patch_area, cohort_traits, cell_forcing, disturb_weight, transitions, land_source, pair_share, river_target, downstream_step, river_water, river_rates, capacity):
    device_count = N_COMP * N_CELL
    mass_blocks = biomass.reshape(P_SIZE, K, device_count, LC).transpose(2, 0, 1, 3)
    area_blocks = patch_area.reshape(P_SIZE, device_count, LC).transpose(1, 0, 2)
    forcing_blocks = cell_forcing.reshape(5, device_count, LC).transpose(1, 0, 2)
    weight_blocks = disturb_weight.reshape(TYPES, device_count, LC).transpose(1, 0, 2)

    def land_block(inputs):
        mass_block, area_block, forcing_block, weight_block = inputs
        grown_mass, runoff_block = canopy(mass_block, area_block, cohort_traits, forcing_block)
        return transit(grown_mass, weight_block, transitions), runoff_block

    transited, runoff_blocks = lax.map(land_block, (mass_blocks, area_blocks, forcing_blocks, weight_blocks))
    runoff = runoff_blocks.transpose(1, 0, 2).reshape(3, LAND)

    device_rows = jnp.arange(device_count, dtype=jnp.int32)
    source_rows = land_source.reshape(device_count, device_count, SLOT)
    share_rows = pair_share.reshape(device_count, device_count, SLOT)
    is_live = source_rows >= 0
    land_cell = jnp.where(is_live, device_rows[:, None, None] * LC + source_rows, 0).astype(jnp.int32)
    pair_values = jnp.where(is_live[None], share_rows[None] * runoff[:, land_cell], 0.0)
    target_rows = river_target.reshape(device_count, device_count, SLOT).transpose(1, 0, 2)
    has_target = target_rows >= 0
    river_cell = jnp.where(has_target, device_rows[None, :, None] * RC + target_rows, RIVER).astype(jnp.int32)
    runoff_in = jnp.stack([jax.ops.segment_sum(pair_values[feature].reshape(-1), river_cell.reshape(-1), num_segments=RIVER + 1)[:RIVER] for feature in range(3)])

    cell_index = jnp.arange(RIVER, dtype=jnp.int32)
    down_cell = jnp.where(downstream_step > 0, cell_index + downstream_step, RIVER).astype(jnp.int32)
    fraction = 1.0 / NSUB
    surface_in = fraction * runoff_in[0:2]
    deep_in = jnp.stack([fraction * runoff_in[2], jnp.zeros_like(runoff_in[2])])
    hill_rate = river_rates[0:2]
    channel_rate = river_rates[2:4]

    def substep(sub_index, state_pair):
        hill_water, channel = state_pair
        hill_out = hill_rate * hill_water
        outflow = channel_rate * channel
        inflow = jnp.stack([jax.ops.segment_sum(outflow[tracer], down_cell, num_segments=RIVER + 1)[:RIVER] for tracer in range(2)])
        return (hill_water - hill_out + surface_in, channel - outflow + hill_out + inflow + deep_in)

    hill_water, channel = lax.fori_loop(0, NSUB, substep, (river_water[0:2], river_water[2:4]))
    stored_total = channel[0] + channel[1]
    inundation = stored_total / (stored_total + capacity)
    flood_back = jnp.where(has_target, inundation[jnp.where(has_target, river_cell, 0)], 0.0)
    flooded = jax.ops.segment_sum((share_rows * flood_back).reshape(-1), jnp.where(is_live, land_cell, LAND).reshape(-1), num_segments=LAND + 1)[:LAND]
    survival = jnp.exp(-cohort_traits[3][None, None, :, None] * flooded.reshape(device_count, LC)[:, None, None, :])
    new_biomass = (transited * survival).transpose(1, 2, 0, 3).reshape(P_SIZE, K, LAND)
    river_state = jnp.concatenate([hill_water, channel], axis=0)
    return new_biomass, flooded, river_state
```

```python
import functools
import math

import jax
import jax.numpy as jnp
from jax import lax
from jax.experimental import pallas as pl
from jax.experimental.pallas import tpu as pltpu
from jax.sharding import PartitionSpec as P

NSUB = 12
LANES = 128
GROUP = 4
F32 = jnp.float32
BF16 = jnp.bfloat16

VMEM = pl.BlockSpec(memory_space=pltpu.VMEM)
SMEM = pl.BlockSpec(memory_space=pltpu.SMEM)


def lane_iota(shape):
    return lax.broadcasted_iota(jnp.int32, shape, len(shape) - 1)


def row_iota(shape):
    return lax.broadcasted_iota(jnp.int32, shape, 0)


def nt_dot(a, b):
    return lax.dot_general(a, b, (((1,), (1,)), ((), ())), preferred_element_type=F32)


def split2(x):
    high = x.astype(BF16).astype(F32)
    return high, x - high


def by_peer(ref, peers, slots):
    rows = ref.shape[0]
    per = peers // rows
    value = ref[...]
    spread = jnp.concatenate(
        [jnp.broadcast_to(value[a : a + 1, :], (per, LANES)) for a in range(rows)], axis=0
    )
    shape = (peers, LANES)
    index = (row_iota(shape) % per) * slots + lane_iota(shape) % slots
    return jnp.take_along_axis(spread, index, axis=1, mode="promise_in_bounds")


def from_peers(ref, rows, slots, feature=None):
    peers = ref.shape[0]
    per = peers // rows
    section = lane_iota((rows, LANES)) // slots
    out = jnp.zeros((rows, LANES), F32)
    for b in range(per):
        part = ref[pl.ds(b, rows, stride=per), :]
        if feature is not None:
            shift = ((b - feature) * slots) % LANES
            if shift:
                part = pltpu.roll(part, shift, 1)
        out = jnp.where(section == b, part, out)
    return out


def statics_kernel(step_ref, rate_ref, out_ref):
    chunks = step_ref.shape[0]
    shape = (chunks, LANES)
    step = step_ref[...]
    cell = row_iota(shape) * LANES + lane_iota(shape)
    target = jnp.where(step > 0, cell + step, -1).astype(F32)
    peers = out_ref.shape[0]
    rates = []
    for q in range(2):
        row = rate_ref[2 + q : 3 + q, :]
        rates.append(
            jnp.concatenate([row[:, h * LANES : (h + 1) * LANES] for h in range(chunks)], axis=0)
        )

    def body(j, carry):
        out_ref[j, 0] = target
        out_ref[j, 1] = rates[0]
        out_ref[j, 2] = rates[1]
        return carry

    lax.fori_loop(0, peers, body, 0)


def rain_kernel(bins, slots, trait_ref, bio_ref, area_ref, force_ref, source_ref, share_ref, out_ref, total_ref):
    step = pl.program_id(0)
    patches = area_ref.shape[0]
    light = force_ref[0:1, :]
    light = light / (light + 0.5)

    @pl.when(step == 0)
    def _():
        total_ref[...] = jnp.zeros_like(total_ref)

    above = jnp.zeros((patches, LANES), F32)
    total = jnp.zeros((patches, LANES), F32)
    for k in reversed(range(bins)):
        leaf = bio_ref[pl.ds(k, patches, stride=bins), :] * trait_ref[0, k]
        total = total + trait_ref[1, k] * leaf * jnp.exp(-0.05 * above)
        above = above + leaf
    total_ref[...] += jnp.sum(total * light * area_ref[...], axis=0, keepdims=True)

    @pl.when(step == pl.num_programs(0) - 1)
    def _():
        peers = out_ref.shape[0]
        shape = (peers, LANES)
        wet = force_ref[1:2, :] * force_ref[2:3, :]
        frozen = force_ref[4:5, :]
        runoff = [
            wet * (1.0 - frozen),
            wet * frozen,
            force_ref[3:4, :] * jnp.exp(-0.5 * (0.5 * total_ref[...])),
        ]
        source = by_peer(source_ref, peers, slots)
        share = by_peer(share_ref, peers, slots)
        safe = jnp.maximum(source, 0)
        section = lane_iota(shape) // slots
        value = jnp.zeros(shape, F32)
        for f in range(3):
            taken = jnp.take_along_axis(
                jnp.broadcast_to(runoff[f], shape), safe, axis=1, mode="promise_in_bounds"
            )
            value = jnp.where(section == f, taken, value)
        out_ref[...] = jnp.where(source >= 0, share * value, 0.0)


def transit_kernel(kinds, bins, trait_ref, trans_ref, bio_ref, force_ref, weight_ref, out_ref, left_ref):
    patches = trans_ref.shape[1]
    rows = kinds * patches
    high, low = split2(trans_ref[...])
    left_ref[:, 0:patches] = high.astype(BF16)
    left_ref[:, patches : 2 * patches] = high.astype(BF16)
    left_ref[:, 2 * patches : 3 * patches] = low.astype(BF16)
    light = force_ref[0:1, :]
    light = light / (light + 0.5)
    weights = [jnp.broadcast_to(weight_ref[t : t + 1, :], (patches, LANES)) for t in range(kinds)]
    half = 0.5 * light

    def one(k, above):
        mass = bio_ref[pl.ds(k, patches, stride=bins), :]
        leaf = mass * trait_ref[0, k]
        gain = trait_ref[1, k] * leaf * jnp.exp(-0.05 * above) * half
        grown = mass * (1.0 - 0.1 * trait_ref[2, k]) + gain
        high, low = split2(grown)
        high = high.astype(BF16)
        return jnp.concatenate([high, low.astype(BF16), high], axis=0), above + leaf

    def body(i, above):
        k = bins - 1 - 2 * i
        first, above = one(k, above)
        second, above = one(k - 1, above)
        right = jnp.concatenate([first, second], axis=1)
        moved = jnp.dot(left_ref[...], right, preferred_element_type=F32)
        for j in range(2):
            part = moved[:, j * LANES : (j + 1) * LANES]
            total = part[0:patches] * weights[0]
            for t in range(1, kinds):
                total = total + part[t * patches : (t + 1) * patches] * weights[t]
            out_ref[pl.ds(k - j, patches, stride=bins), :] = total
        return above

    lax.fori_loop(0, bins // 2, body, jnp.zeros((patches, LANES), F32), unroll=4)


def river_kernel(
    slots,
    here_ref,
    static_ref,
    arrived_ref,
    target_ref,
    water_ref,
    rate_ref,
    out_ref,
    hill_out_ref,
    lo_ref,
    mask_ref,
    state_ref,
    speed_ref,
    value_ref,
    left_ref,
    rows_left_ref,
    rows_lo_ref,
    hill_ref,
    hill_rate_ref,
    force_ref,
):
    peers = static_ref.shape[0]
    chunks = static_ref.shape[2]
    spans = 2 * chunks
    window = state_ref.shape[0]
    here = here_ref[0]
    rows = target_ref.shape[0]

    def block_of(b):
        j = here + b
        return jnp.where(j >= peers, j - peers, j)

    def table(b, carry):
        j = block_of(b)
        target = static_ref[j, 0].astype(jnp.int32)
        span = target >> 7
        low = target & 127
        for h in range(chunks):
            at = slice(h * LANES, (h + 1) * LANES)
            mask_ref[b, :, at] = jnp.where(
                row_iota((spans, LANES)) == span[h : h + 1, :], 1.0, 0.0
            ).astype(BF16)
            lo_ref[b, :, at] = jnp.where(
                row_iota((LANES, LANES)) == low[h : h + 1, :], 1.0, 0.0
            ).astype(BF16)
        speed_ref[b, 0] = static_ref[j, 1]
        speed_ref[b, 1] = static_ref[j, 2]
        return carry

    lax.fori_loop(0, window - 1, table, 0)

    target = target_ref[...]
    span = target >> 7
    low = target & 127
    values = []
    for f in range(3):
        values.append(split2(from_peers(arrived_ref, rows, slots, f)))
    for a in range(rows):
        at = slice(a * LANES, (a + 1) * LANES)
        mask = row_iota((chunks, LANES)) == span[a : a + 1, :]
        for s in range(2):
            for f in range(3):
                m = (s * 3 + f) * chunks
                rows_left_ref[m : m + chunks, at] = jnp.where(
                    mask, values[f][s][a : a + 1, :], 0.0
                ).astype(BF16)
        rows_lo_ref[:, at] = jnp.where(
            row_iota((LANES, LANES)) == low[a : a + 1, :], 1.0, 0.0
        ).astype(BF16)
    taken = nt_dot(rows_left_ref[...], rows_lo_ref[...])
    fraction = 1.0 / NSUB
    half = 3 * chunks
    for f in range(3):
        force_ref[f] = fraction * (
            taken[f * chunks : (f + 1) * chunks] + taken[half + f * chunks : half + (f + 1) * chunks]
        )

    state_ref[...] = jnp.zeros_like(state_ref)
    for q in range(2):
        for h in range(chunks):
            at = slice(h * LANES, (h + 1) * LANES)
            hill_ref[q, h : h + 1, :] = water_ref[q : q + 1, at]
            hill_rate_ref[q, h : h + 1, :] = rate_ref[q : q + 1, at]
            state_ref[0, q, h : h + 1, :] = water_ref[2 + q : 3 + q, at]

    def outflow_of(b, g):
        outs = []
        for q in range(2):
            out = speed_ref[b, q] * state_ref[b, q]
            high, lowp = split2(out)
            value_ref[g, q] = high
            value_ref[g, 2 + q] = lowp
            outs.append(out)
        for h in range(chunks):
            at = slice(h * LANES, (h + 1) * LANES)
            mask = mask_ref[b, :, at]
            for sq in range(4):
                row = jnp.broadcast_to(value_ref[g, sq, h : h + 1, :], (spans, LANES))
                left_ref[g, sq * spans : (sq + 1) * spans, at] = row.astype(BF16) * mask
        return outs

    def group_step(first):
        outs = [outflow_of(first + g, g) for g in range(GROUP)]
        flows = [nt_dot(left_ref[g], lo_ref[first + g]) for g in range(GROUP)]
        for q in range(2):
            carried = None
            for g in range(GROUP):
                flow = flows[g][q * spans : (q + 1) * spans] + flows[g][(2 + q) * spans : (3 + q) * spans]
                new = state_ref[first + g, q] - outs[g][q] + flow[0:chunks]
                if carried is not None:
                    new = new + carried
                state_ref[first + g, q] = new
                carried = flow[chunks:spans]
            state_ref[first + GROUP, q] += carried

    for phase in range(NSUB // GROUP):

        def step(t, carry):
            for group in reversed(range(phase + 1)):
                group_step(group * GROUP)
            for q in range(2):
                hill = hill_ref[q]
                gone = hill_rate_ref[q] * hill
                add = gone + force_ref[2] if q == 0 else gone
                state_ref[0, q] += add
                hill_ref[q] = hill - gone + force_ref[q]
            return carry

        lax.fori_loop(0, GROUP, step, 0)

    hill_out_ref[...] = hill_ref[...]

    def send(b, carry):
        out_ref[block_of(b)] = state_ref[b]
        return carry

    lax.fori_loop(0, window, send, 0)


def inundate_kernel(slots, window, here_ref, part_ref, capacity_ref, target_ref, hill_ref, state_ref, back_ref):
    peers = part_ref.shape[0]
    chunks = capacity_ref.shape[0]
    here = here_ref[0]
    channel = jnp.zeros(part_ref.shape[1:], F32)
    for b in range(window):
        j = here - b
        j = jnp.where(j < 0, j + peers, j)
        channel = channel + part_ref[j]
    for q in range(2):
        for h in range(chunks):
            at = slice(h * LANES, (h + 1) * LANES)
            state_ref[q : q + 1, at] = hill_ref[q, h : h + 1, :]
            state_ref[2 + q : 3 + q, at] = channel[q, h : h + 1, :]
    stored = channel[0] + channel[1]
    wet = stored / (stored + capacity_ref[...])
    target = by_peer(target_ref, peers, slots)
    span = target >> 7
    low = target & 127
    back = jnp.zeros((peers, LANES), F32)
    for h in range(chunks):
        taken = jnp.take_along_axis(
            jnp.broadcast_to(wet[h : h + 1, :], (peers, LANES)), low, axis=1, mode="promise_in_bounds"
        )
        back = jnp.where(span == h, taken, back)
    back_ref[...] = back


def survive_kernel(bins, slots, trait_ref, back_ref, share_ref, source_ref, moved_ref, out_ref, flooded_ref, alive_ref):
    @pl.when(pl.program_id(0) == 0)
    def _():
        rows = share_ref.shape[0]
        value = share_ref[...] * from_peers(back_ref, rows, slots)
        source = source_ref[...]
        total = jnp.zeros((LANES, LANES), F32)
        for a in range(rows):
            total = total + jnp.where(
                row_iota((LANES, LANES)) == source[a : a + 1, :], value[a : a + 1, :], 0.0
            )
        flooded = jnp.sum(total.T, axis=0, keepdims=True)
        flooded_ref[...] = flooded
        for k in range(bins):
            alive_ref[k : k + 1, :] = jnp.exp(-trait_ref[3, k] * flooded)

    alive = alive_ref[...]
    for p in range(moved_ref.shape[0] // bins):
        at = slice(p * bins, (p + 1) * bins)
        out_ref[at, :] = moved_ref[at, :] * alive


def shards(
    axes,
    biomass,
    patch_area,
    cohort_traits,
    cell_forcing,
    disturb_weight,
    transitions,
    land_source,
    pair_share,
    river_target,
    downstream_step,
    river_water,
    river_rates,
    capacity,
):
    patches, bins, lands = biomass.shape
    rivers = river_water.shape[1]
    peers = math.prod(lax.axis_size(a) for a in axes)
    slots = land_source.shape[0] // peers
    rows = land_source.shape[0] // LANES
    chunks = rivers // LANES
    kinds = transitions.shape[0]
    window = NSUB + 1
    here = lax.axis_index(axes).astype(jnp.int32).reshape(1)

    bio = biomass.reshape(patches * bins, lands)
    source = land_source.reshape(rows, LANES)
    share = pair_share.reshape(rows, LANES)
    target = river_target.reshape(rows, LANES)
    step = downstream_step.reshape(chunks, LANES)

    statics = pl.pallas_call(
        statics_kernel,
        out_shape=jax.ShapeDtypeStruct((peers, 3, chunks, LANES), F32),
        in_specs=[VMEM, VMEM],
        out_specs=VMEM,
        name="statics",
    )(step, river_rates)
    statics = lax.all_to_all(statics, axes, split_axis=0, concat_axis=0, tiled=True)

    tile = 16
    message = pl.pallas_call(
        functools.partial(rain_kernel, bins, slots),
        grid=(patches // tile,),
        out_shape=jax.ShapeDtypeStruct((peers, LANES), F32),
        in_specs=[
            SMEM,
            pl.BlockSpec((tile * bins, LANES), lambda i: (i, 0)),
            pl.BlockSpec((tile, LANES), lambda i: (i, 0)),
            pl.BlockSpec((5, LANES), lambda i: (0, 0)),
            pl.BlockSpec((rows, LANES), lambda i: (0, 0)),
            pl.BlockSpec((rows, LANES), lambda i: (0, 0)),
        ],
        out_specs=pl.BlockSpec((peers, LANES), lambda i: (0, 0)),
        scratch_shapes=[pltpu.VMEM((1, LANES), F32)],
        name="rain",
    )(cohort_traits, bio, patch_area, cell_forcing, source, share)
    arrived = lax.all_to_all(message, axes, split_axis=0, concat_axis=0, tiled=True)

    moved = pl.pallas_call(
        functools.partial(transit_kernel, kinds, bins),
        out_shape=jax.ShapeDtypeStruct((patches * bins, LANES), F32),
        in_specs=[SMEM, VMEM, VMEM, VMEM, VMEM],
        out_specs=VMEM,
        scratch_shapes=[pltpu.VMEM((kinds * patches, 3 * patches), BF16)],
        name="transit",
    )(cohort_traits, transitions.reshape(kinds * patches, patches), bio, cell_forcing, disturb_weight)

    spans = 2 * chunks
    parts, hill = pl.pallas_call(
        functools.partial(river_kernel, slots),
        out_shape=(
            jax.ShapeDtypeStruct((peers, 2, chunks, LANES), F32),
            jax.ShapeDtypeStruct((2, chunks, LANES), F32),
        ),
        in_specs=[SMEM] + [VMEM] * 5,
        out_specs=(VMEM, VMEM),
        scratch_shapes=[
            pltpu.VMEM((window - 1, LANES, rivers), BF16),
            pltpu.VMEM((window - 1, spans, rivers), BF16),
            pltpu.VMEM((window, 2, chunks, LANES), F32),
            pltpu.VMEM((window - 1, 2, chunks, LANES), F32),
            pltpu.VMEM((GROUP, 4, chunks, LANES), F32),
            pltpu.VMEM((GROUP, 4 * spans, rivers), BF16),
            pltpu.VMEM((6 * chunks, rows * LANES), BF16),
            pltpu.VMEM((LANES, rows * LANES), BF16),
            pltpu.VMEM((2, chunks, LANES), F32),
            pltpu.VMEM((2, chunks, LANES), F32),
            pltpu.VMEM((3, chunks, LANES), F32),
        ],
        name="river",
    )(here, statics, arrived, target, river_water, river_rates)
    parts = lax.all_to_all(parts, axes, split_axis=0, concat_axis=0, tiled=True)

    river_state, back = pl.pallas_call(
        functools.partial(inundate_kernel, slots, window),
        out_shape=(
            jax.ShapeDtypeStruct((4, rivers), F32),
            jax.ShapeDtypeStruct((peers, LANES), F32),
        ),
        in_specs=[SMEM] + [VMEM] * 4,
        out_specs=(VMEM, VMEM),
        name="inundate",
    )(here, parts, capacity.reshape(chunks, LANES), target, hill)
    back = lax.all_to_all(back, axes, split_axis=0, concat_axis=0, tiled=True)

    tile = 12
    new_biomass, flooded = pl.pallas_call(
        functools.partial(survive_kernel, bins, slots),
        grid=(patches // tile,),
        out_shape=(
            jax.ShapeDtypeStruct((patches * bins, LANES), F32),
            jax.ShapeDtypeStruct((1, LANES), F32),
        ),
        in_specs=[
            SMEM,
            pl.BlockSpec((peers, LANES), lambda i: (0, 0)),
            pl.BlockSpec((rows, LANES), lambda i: (0, 0)),
            pl.BlockSpec((rows, LANES), lambda i: (0, 0)),
            pl.BlockSpec((tile * bins, LANES), lambda i: (i, 0)),
        ],
        out_specs=(
            pl.BlockSpec((tile * bins, LANES), lambda i: (i, 0)),
            pl.BlockSpec((1, LANES), lambda i: (0, 0)),
        ),
        scratch_shapes=[pltpu.VMEM((bins, LANES), F32)],
        name="survive",
    )(cohort_traits, back, share, source, moved)
    return (new_biomass.reshape(patches, bins, lands), flooded.reshape(lands), river_state)


def solution(mesh):
    axes = tuple(mesh.axis_names)
    split = P(axes)
    split1 = P(None, axes)
    return jax.shard_map(
        functools.partial(shards, axes),
        mesh=mesh,
        in_specs=(
            P(None, None, axes),
            split1,
            P(),
            split1,
            split1,
            P(),
            split,
            split,
            split,
            split,
            split1,
            split1,
            split,
        ),
        out_specs=(P(None, None, axes), split, split1),
        check_vma=False,
    )
```

```python
import functools
import math

import jax
import jax.numpy as jnp
from jax import lax
from jax.experimental import pallas as pl
from jax.experimental.pallas import tpu as pltpu
from jax.sharding import PartitionSpec as P


NSUB = 12
LANES = 128
PHASE = 2
F32 = jnp.float32
BF16 = jnp.bfloat16

VMEM = pl.BlockSpec(memory_space=pltpu.VMEM)
ANY = pl.BlockSpec(memory_space=pl.ANY)
SMEM = pl.BlockSpec(memory_space=pltpu.SMEM)


def lane_iota(shape):
    return lax.broadcasted_iota(jnp.int32, shape, len(shape) - 1)


def row_iota(shape):
    return lax.broadcasted_iota(jnp.int32, shape, 0)


def nt_dot(a, b):
    return lax.dot_general(a, b, (((1,), (1,)), ((), ())), preferred_element_type=F32)


def split2(x):
    high = x.astype(BF16).astype(F32)
    return high, x - high


def by_peer(ref, peers, slots):
    rows = ref.shape[0]
    per = peers // rows
    value = ref[...]
    spread = jnp.concatenate(
        [jnp.broadcast_to(value[a : a + 1, :], (per, LANES)) for a in range(rows)], axis=0
    )
    shape = (peers, LANES)
    index = (row_iota(shape) % per) * slots + lane_iota(shape) % slots
    return jnp.take_along_axis(spread, index, axis=1, mode="promise_in_bounds")


def from_peers(ref, rows, slots, feature=None, which=0, count=1):
    peers = ref.shape[0] // count
    per = peers // rows
    section = lane_iota((rows, LANES)) // slots
    out = jnp.zeros((rows, LANES), F32)
    for b in range(per):
        part = ref[pl.ds(b * count + which, rows, stride=per * count), :]
        if feature is not None:
            shift = ((b - feature) * slots) % LANES
            if shift:
                part = pltpu.roll(part, shift, 1)
        out = jnp.where(section == b, part, out)
    return out


def unrow(row, chunks):
    return jnp.concatenate([row[:, h * LANES : (h + 1) * LANES] for h in range(chunks)], axis=0)


def rain_kernel(
    bins,
    slots,
    core_ref,
    trait_ref,
    bio_ref,
    area_ref,
    force_ref,
    source_ref,
    share_ref,
    step_ref,
    target_ref,
    water_ref,
    rate_ref,
    out_ref,
    mate_ref,
    total_ref,
    static_ref,
    rows_ref,
    sems,
    rows_sem,
):
    step = pl.program_id(0)
    patches = area_ref.shape[0]
    peers = out_ref.shape[0]
    chunks = step_ref.shape[0]
    light = force_ref[0:1, :]
    light = light / (light + 0.5)

    def spread(j):
        return pltpu.make_async_copy(
            static_ref.at[j % 2], out_ref.at[j, pl.ds(0, 2 * chunks)], sems.at[j]
        )

    @pl.when(step == 0)
    def _():
        total_ref[...] = jnp.zeros_like(total_ref)
        shape = (chunks, LANES)
        moves = step_ref[...]
        cell = row_iota(shape) * LANES + lane_iota(shape)
        target = jnp.where(moves > 0, cell + moves, -1).astype(F32)
        for q in range(2):
            static_ref[q, 0:chunks, :] = target
            static_ref[q, chunks : 2 * chunks, :] = unrow(rate_ref[2 + q : 3 + q, :], chunks)
        for j in range(peers):
            spread(j).start()
        first = core_ref[0] == 0
        for i, (ref, at) in enumerate(((water_ref, 2), (water_ref, 0), (rate_ref, 0))):
            other = jnp.where(first, ref[at + 1 : at + 2, :], ref[at : at + 1, :])
            mate_ref[i * chunks : (i + 1) * chunks, :] = unrow(other, chunks)
        mate_ref[3 * chunks :, :] = target_ref[...].astype(F32)

    above = jnp.zeros((patches, LANES), F32)
    total = jnp.zeros((patches, LANES), F32)
    for k in reversed(range(bins)):
        leaf = bio_ref[pl.ds(k, patches, stride=bins), :] * trait_ref[0, k]
        total = total + trait_ref[1, k] * leaf * jnp.exp(-0.05 * above)
        above = above + leaf
    total_ref[...] += jnp.sum(total * light * area_ref[...], axis=0, keepdims=True)

    @pl.when(step == pl.num_programs(0) - 1)
    def _():
        shape = (peers, LANES)
        wet = force_ref[1:2, :] * force_ref[2:3, :]
        frozen = force_ref[4:5, :]
        runoff = [
            wet * (1.0 - frozen),
            wet * frozen,
            force_ref[3:4, :] * jnp.exp(-0.5 * (0.5 * total_ref[...])),
        ]
        source = by_peer(source_ref, peers, slots)
        share = by_peer(share_ref, peers, slots)
        safe = jnp.maximum(source, 0)
        section = lane_iota(shape) // slots
        value = jnp.zeros(shape, F32)
        for f in range(3):
            taken = jnp.take_along_axis(
                jnp.broadcast_to(runoff[f], shape), safe, axis=1, mode="promise_in_bounds"
            )
            value = jnp.where(section == f, taken, value)
        own = jnp.where(source >= 0, share * value, 0.0)
        mate = jnp.where(
            row_iota(shape) % 2 == 0, pltpu.roll(own, peers - 1, 0), pltpu.roll(own, 1, 0)
        )
        rows_ref[pl.ds(0, peers, stride=8), :] = own
        rows_ref[pl.ds(1, peers, stride=8), :] = mate
        copy = pltpu.make_async_copy(
            rows_ref.reshape(peers, 8, LANES), out_ref.at[:, pl.ds(2 * chunks, 8)], rows_sem
        )
        copy.start()
        for j in range(peers):
            spread(j).wait()
        copy.wait()


def transit_kernel(kinds, bins, trait_ref, trans_ref, bio_ref, force_ref, weight_ref, out_ref, left_ref):
    patches = trans_ref.shape[1]
    high, low = split2(trans_ref[...])
    left_ref[:, 0:patches] = high.astype(BF16)
    left_ref[:, patches : 2 * patches] = high.astype(BF16)
    left_ref[:, 2 * patches : 3 * patches] = low.astype(BF16)
    light = force_ref[0:1, :]
    light = light / (light + 0.5)
    weights = [jnp.broadcast_to(weight_ref[t : t + 1, :], (patches, LANES)) for t in range(kinds)]
    half = 0.5 * light

    def one(k, above):
        mass = bio_ref[pl.ds(k, patches, stride=bins), :]
        leaf = mass * trait_ref[0, k]
        gain = trait_ref[1, k] * leaf * jnp.exp(-0.05 * above) * half
        grown = mass * (1.0 - 0.1 * trait_ref[2, k]) + gain
        high, low = split2(grown)
        high = high.astype(BF16)
        return jnp.concatenate([high, low.astype(BF16), high], axis=0), above + leaf

    def body(i, above):
        k = bins - 1 - 2 * i
        first, above = one(k, above)
        second, above = one(k - 1, above)
        right = jnp.concatenate([first, second], axis=1)
        moved = jnp.dot(left_ref[...], right, preferred_element_type=F32)
        for j in range(2):
            part = moved[:, j * LANES : (j + 1) * LANES]
            total = part[0:patches] * weights[0]
            for t in range(1, kinds):
                total = total + part[t * patches : (t + 1) * patches] * weights[t]
            out_ref[pl.ds(k - j, patches, stride=bins), :] = total
        return above

    lax.fori_loop(0, bins // 2, body, jnp.zeros((patches, LANES), F32), unroll=4)


def river_kernel(
    slots,
    here_ref,
    arrived_ref,
    target_ref,
    mate_ref,
    water_ref,
    rate_ref,
    out_ref,
    hill_out_ref,
    lo_ref,
    mask_ref,
    state_ref,
    speed_ref,
    value_ref,
    rows_left_ref,
    rows_lo_ref,
    hill_ref,
    hill_rate_ref,
    runoff_ref,
    sems,
):
    peers = arrived_ref.shape[0]
    chunks = state_ref.shape[1]
    spans = 2 * chunks
    window = state_ref.shape[0]
    base = here_ref[0]
    core = here_ref[1]
    other = 1 - core
    rows = target_ref.shape[0]

    def block_of(b):
        j = base + b
        return jnp.where(j >= peers, j - peers, j)

    square = (LANES, LANES)
    eye = jnp.where(row_iota(square) == lane_iota(square), 1.0, 0.0).astype(BF16)
    wide = (2 * LANES, 2 * LANES)
    ones = jnp.where(row_iota(wide) // LANES == lane_iota(wide) // LANES, 1.0, 0.0).astype(BF16)
    lane = lane_iota(square).astype(F32)

    def table(b, carry):
        j = block_of(b)
        target = arrived_ref[j, 0:chunks].astype(jnp.int32)
        span = target >> 7
        low = (target & 127).astype(F32)
        for h in range(0, chunks, 2):
            diagonal = jnp.concatenate(
                [
                    jnp.broadcast_to(low[h + i : h + i + 1, :], square).astype(BF16) * eye
                    for i in range(2)
                ],
                axis=1,
            )
            column = jnp.dot(diagonal, ones, preferred_element_type=F32)
            for i in range(2):
                at = slice((h + i) * LANES, (h + i + 1) * LANES)
                mask_ref[b, h + i] = jnp.where(
                    row_iota((spans, LANES)) == span[h + i : h + i + 1, :], 1.0, 0.0
                ).astype(BF16)
                lo_ref[b, at, :] = jnp.where(
                    column[:, i * LANES : (i + 1) * LANES] == lane, 1.0, 0.0
                ).astype(BF16)
        speed_ref[b] = arrived_ref[j, chunks:spans]
        return carry

    lax.fori_loop(0, window - 1, table, 0)

    arrived_rows_ref = arrived_ref.reshape(peers * arrived_ref.shape[1], LANES)
    fraction = 1.0 / NSUB
    half = 3 * chunks
    for which in range(2):
        if which == 0:
            target = target_ref[...]
        else:
            target = mate_ref[3 * chunks :, :].astype(jnp.int32)
        span = target >> 7
        low = target & 127
        values = [split2(from_peers(arrived_rows_ref, rows, slots, f, spans + which, arrived_ref.shape[1])) for f in range(3)]
        for a in range(rows):
            mask = row_iota((chunks, LANES)) == span[a : a + 1, :]
            for s in range(2):
                for f in range(3):
                    m = (s * 3 + f) * chunks
                    rows_left_ref[which, a, m : m + chunks, :] = jnp.where(
                        mask, values[f][s][a : a + 1, :], 0.0
                    ).astype(BF16)
            rows_lo_ref[which, a] = jnp.where(
                row_iota((LANES, LANES)) == low[a : a + 1, :], 1.0, 0.0
            ).astype(BF16)
        taken = nt_dot(
            jnp.concatenate([rows_left_ref[which, a] for a in range(rows)], axis=1),
            jnp.concatenate([rows_lo_ref[which, a] for a in range(rows)], axis=1),
        )
        for f in range(3):
            runoff_ref[which, f] = fraction * (
                taken[f * chunks : (f + 1) * chunks]
                + taken[half + f * chunks : half + (f + 1) * chunks]
            )

    state_ref[...] = jnp.zeros_like(state_ref)
    for q in range(2):
        hill_ref[q] = unrow(water_ref[q : q + 1, :], chunks)
        hill_rate_ref[q] = unrow(rate_ref[q : q + 1, :], chunks)
    own = jnp.where(core == 0, water_ref[2:3, :], water_ref[3:4, :])
    state_ref[core] = unrow(own, chunks)
    state_ref[other] = mate_ref[0:chunks, :]
    hill_ref[2] = mate_ref[chunks : 2 * chunks, :]
    hill_rate_ref[2] = mate_ref[2 * chunks : 3 * chunks, :]
    deep = [jnp.where(core == 0, runoff_ref[which, 2], 0.0) for which in range(2)]
    surface = [runoff_ref[0, 0], runoff_ref[0, 1], runoff_ref[1, core]]

    def block_flow(b):
        out = speed_ref[b] * state_ref[b]
        high, low = split2(out)
        value_ref[b, 0] = high
        value_ref[b, 1] = low
        pieces = []
        for h in range(chunks):
            mask = mask_ref[b, h]
            pieces.append(
                jnp.concatenate(
                    [
                        jnp.broadcast_to(value_ref[b, s, h : h + 1, :], (spans, LANES)).astype(BF16)
                        * mask
                        for s in range(2)
                    ],
                    axis=0,
                )
            )
        flow = jnp.dot(
            jnp.concatenate(pieces, axis=1), lo_ref[b], preferred_element_type=F32
        )
        return out, flow[0:spans] + flow[spans : 2 * spans]

    def advance(count):
        for b in reversed(range(count)):
            out, flow = block_flow(b)
            state_ref[b] = state_ref[b] - out + flow[0:chunks]
            state_ref[b + 1] += flow[chunks:spans]

    for phase in range(NSUB // PHASE):

        def step(t, carry):
            advance(phase * PHASE + PHASE + 1)
            gone = [hill_rate_ref[i] * hill_ref[i] for i in range(3)]
            for i in range(3):
                hill_ref[i] = hill_ref[i] - gone[i] + surface[i]
            state_ref[core] += jnp.where(core == 0, gone[0], gone[1]) + deep[0]
            state_ref[other] += gone[2] + deep[1]
            return carry

        lax.fori_loop(0, PHASE, step, 0)

    hill_out_ref[...] = hill_ref[0:2]

    def send(b):
        return pltpu.make_async_copy(state_ref.at[b], out_ref.at[block_of(b)], sems.at[b])

    for b in range(window):
        send(b).start()
    for b in range(window):
        send(b).wait()


def inundate_kernel(slots, window, here_ref, part_ref, capacity_ref, target_ref, hill_ref, state_ref, back_ref):
    peers = part_ref.shape[0]
    chunks = capacity_ref.shape[0]
    channel = [jnp.zeros(part_ref.shape[1:], F32)] * 2
    for b in range(0, window, 2):
        j = here_ref[0] - b
        j = jnp.where(j < 0, j + peers, j)
        for q in range(2):
            channel[q] = channel[q] + part_ref[j + q]
    for q in range(2):
        for h in range(chunks):
            at = slice(h * LANES, (h + 1) * LANES)
            state_ref[q : q + 1, at] = hill_ref[q, h : h + 1, :]
            state_ref[2 + q : 3 + q, at] = channel[q][h : h + 1, :]
    stored = channel[0] + channel[1]
    wet = stored / (stored + capacity_ref[...])
    target = by_peer(target_ref, peers, slots)
    span = target >> 7
    low = target & 127
    back = jnp.zeros((peers, LANES), F32)
    for h in range(chunks):
        taken = jnp.take_along_axis(
            jnp.broadcast_to(wet[h : h + 1, :], (peers, LANES)), low, axis=1, mode="promise_in_bounds"
        )
        back = jnp.where(span == h, taken, back)
    back_ref[...] = back


def survive_kernel(bins, slots, trait_ref, back_ref, share_ref, source_ref, moved_ref, out_ref, flooded_ref, alive_ref):
    @pl.when(pl.program_id(0) == 0)
    def _():
        rows = share_ref.shape[0]
        value = share_ref[...] * from_peers(back_ref, rows, slots)
        source = source_ref[...]
        total = jnp.zeros((LANES, LANES), F32)
        for a in range(rows):
            total = total + jnp.where(
                row_iota((LANES, LANES)) == source[a : a + 1, :], value[a : a + 1, :], 0.0
            )
        flooded = jnp.sum(total.T, axis=0, keepdims=True)
        flooded_ref[...] = flooded
        for k in range(bins):
            alive_ref[k : k + 1, :] = jnp.exp(-trait_ref[3, k] * flooded)

    alive = alive_ref[...]
    for p in range(moved_ref.shape[0] // bins):
        at = slice(p * bins, (p + 1) * bins)
        out_ref[at, :] = moved_ref[at, :] * alive


def shards(
    axes,
    biomass,
    patch_area,
    cohort_traits,
    cell_forcing,
    disturb_weight,
    transitions,
    land_source,
    pair_share,
    river_target,
    downstream_step,
    river_water,
    river_rates,
    capacity,
):
    patches, bins, lands = biomass.shape
    rivers = river_water.shape[1]
    peers = math.prod(lax.axis_size(a) for a in axes)
    slots = land_source.shape[0] // peers
    rows = land_source.shape[0] // LANES
    chunks = rivers // LANES
    kinds = transitions.shape[0]
    window = NSUB + 2
    place = lax.axis_index(axes).astype(jnp.int32)
    here = jnp.stack([place - place % 2, place % 2])

    bio = biomass.reshape(patches * bins, lands)
    source = land_source.reshape(rows, LANES)
    share = pair_share.reshape(rows, LANES)
    target = river_target.reshape(rows, LANES)
    step = downstream_step.reshape(chunks, LANES)

    tile = 16
    whole = lambda *shape: pl.BlockSpec(shape, lambda i: (0,) * len(shape))
    message, mate = pl.pallas_call(
        functools.partial(rain_kernel, bins, slots),
        grid=(patches // tile,),
        out_shape=(
            jax.ShapeDtypeStruct((peers, 2 * chunks + 8, LANES), F32),
            jax.ShapeDtypeStruct((3 * chunks + rows, LANES), F32),
        ),
        in_specs=[
            SMEM,
            SMEM,
            pl.BlockSpec((tile * bins, LANES), lambda i: (i, 0)),
            pl.BlockSpec((tile, LANES), lambda i: (i, 0)),
            whole(5, LANES),
            whole(rows, LANES),
            whole(rows, LANES),
            whole(chunks, LANES),
            whole(rows, LANES),
            whole(4, rivers),
            whole(4, rivers),
        ],
        out_specs=(ANY, whole(3 * chunks + rows, LANES)),
        scratch_shapes=[
            pltpu.VMEM((1, LANES), F32),
            pltpu.VMEM((2, 2 * chunks, LANES), F32),
            pltpu.VMEM((peers * 8, LANES), F32),
            pltpu.SemaphoreType.DMA((peers,)),
            pltpu.SemaphoreType.DMA(()),
        ],
        name="rain",
    )(
        here[1:2],
        cohort_traits,
        bio,
        patch_area,
        cell_forcing,
        source,
        share,
        step,
        target,
        river_water,
        river_rates,
    )
    arrived = lax.all_to_all(message, axes, split_axis=0, concat_axis=0, tiled=True)
    mate = lax.ppermute(mate, axes, [(i, i + 1 - 2 * (i % 2)) for i in range(peers)])

    moved = pl.pallas_call(
        functools.partial(transit_kernel, kinds, bins),
        out_shape=jax.ShapeDtypeStruct((patches * bins, LANES), F32),
        in_specs=[SMEM, VMEM, VMEM, VMEM, VMEM],
        out_specs=VMEM,
        scratch_shapes=[pltpu.VMEM((kinds * patches, 3 * patches), BF16)],
        name="transit",
    )(cohort_traits, transitions.reshape(kinds * patches, patches), bio, cell_forcing, disturb_weight)

    spans = 2 * chunks
    parts, hill = pl.pallas_call(
        functools.partial(river_kernel, slots),
        out_shape=(
            jax.ShapeDtypeStruct((peers, chunks, LANES), F32),
            jax.ShapeDtypeStruct((2, chunks, LANES), F32),
        ),
        in_specs=[SMEM] + [VMEM] * 5,
        out_specs=(ANY, VMEM),
        scratch_shapes=[
            pltpu.VMEM((window - 1, rivers, LANES), BF16),
            pltpu.VMEM((window - 1, chunks, spans, LANES), BF16),
            pltpu.VMEM((window, chunks, LANES), F32),
            pltpu.VMEM((window - 1, chunks, LANES), F32),
            pltpu.VMEM((window - 1, 2, chunks, LANES), F32),
            pltpu.VMEM((2, rows, 6 * chunks, LANES), BF16),
            pltpu.VMEM((2, rows, LANES, LANES), BF16),
            pltpu.VMEM((3, chunks, LANES), F32),
            pltpu.VMEM((3, chunks, LANES), F32),
            pltpu.VMEM((2, 3, chunks, LANES), F32),
            pltpu.SemaphoreType.DMA((window,)),
        ],
        name="river",
    )(here, arrived, target, mate, river_water, river_rates)
    parts = lax.all_to_all(parts, axes, split_axis=0, concat_axis=0, tiled=True)

    river_state, back = pl.pallas_call(
        functools.partial(inundate_kernel, slots, window),
        out_shape=(
            jax.ShapeDtypeStruct((4, rivers), F32),
            jax.ShapeDtypeStruct((peers, LANES), F32),
        ),
        in_specs=[SMEM] + [VMEM] * 4,
        out_specs=(VMEM, VMEM),
        name="inundate",
    )(here, parts, capacity.reshape(chunks, LANES), target, hill)
    back = lax.all_to_all(back, axes, split_axis=0, concat_axis=0, tiled=True)

    tile = 12
    new_biomass, flooded = pl.pallas_call(
        functools.partial(survive_kernel, bins, slots),
        grid=(patches // tile,),
        out_shape=(
            jax.ShapeDtypeStruct((patches * bins, LANES), F32),
            jax.ShapeDtypeStruct((1, LANES), F32),
        ),
        in_specs=[
            SMEM,
            pl.BlockSpec((peers, LANES), lambda i: (0, 0)),
            pl.BlockSpec((rows, LANES), lambda i: (0, 0)),
            pl.BlockSpec((rows, LANES), lambda i: (0, 0)),
            pl.BlockSpec((tile * bins, LANES), lambda i: (i, 0)),
        ],
        out_specs=(
            pl.BlockSpec((tile * bins, LANES), lambda i: (i, 0)),
            pl.BlockSpec((1, LANES), lambda i: (0, 0)),
        ),
        scratch_shapes=[pltpu.VMEM((bins, LANES), F32)],
        name="survive",
    )(cohort_traits, back, share, source, moved)
    return (new_biomass.reshape(patches, bins, lands), flooded.reshape(lands), river_state)


def solution(mesh):
    axes = tuple(mesh.axis_names)
    split = P(axes)
    split1 = P(None, axes)

    def body(*args):
        return shards(axes, *args)

    return jax.shard_map(
        body,
        mesh=mesh,
        in_specs=(
            P(None, None, axes),
            split1,
            P(),
            split1,
            split1,
            P(),
            split,
            split,
            split,
            split,
            split1,
            split1,
            split,
        ),
        out_specs=(P(None, None, axes), split, split1),
        check_vma=False,
    )
```

```python
import functools
import math

import jax
import jax.numpy as jnp
from jax import lax
from jax.experimental import pallas as pl
from jax.experimental.pallas import tpu as pltpu
from jax.sharding import PartitionSpec as P


NSUB = 12
LANES = 128
PHASE = 2
F32 = jnp.float32
BF16 = jnp.bfloat16

VMEM = pl.BlockSpec(memory_space=pltpu.VMEM)
ANY = pl.BlockSpec(memory_space=pl.ANY)
SMEM = pl.BlockSpec(memory_space=pltpu.SMEM)


def lane_iota(shape):
    return lax.broadcasted_iota(jnp.int32, shape, len(shape) - 1)


def row_iota(shape):
    return lax.broadcasted_iota(jnp.int32, shape, 0)


def nt_dot(a, b):
    return lax.dot_general(a, b, (((1,), (1,)), ((), ())), preferred_element_type=F32)


def split2(x):
    high = x.astype(BF16).astype(F32)
    return high, x - high


def by_peer(value, peers, slots):
    rows = value.shape[0]
    per = peers // rows
    spread = jnp.concatenate(
        [jnp.broadcast_to(value[a : a + 1, :], (per, LANES)) for a in range(rows)], axis=0
    )
    shape = (peers, LANES)
    index = (row_iota(shape) % per) * slots + lane_iota(shape) % slots
    return jnp.take_along_axis(spread, index, axis=1, mode="promise_in_bounds")


def from_peers(ref, rows, slots, feature=None, which=0, count=1):
    peers = ref.shape[0] // count
    per = peers // rows
    section = lane_iota((rows, LANES)) // slots
    out = jnp.zeros((rows, LANES), F32)
    for b in range(per):
        part = ref[pl.ds(b * count + which, rows, stride=per * count), :]
        if feature is not None:
            shift = ((b - feature) * slots) % LANES
            if shift:
                part = pltpu.roll(part, shift, 1)
        out = jnp.where(section == b, part, out)
    return out


def all_sections(value, slots):
    shift = slots
    while shift < LANES:
        value = value + pltpu.roll(value, shift, 1)
        shift *= 2
    return value


def look_up(table, index):
    span = index >> 7
    low = index & 127
    out = jnp.zeros(index.shape, F32)
    for h in range(table.shape[0]):
        taken = jnp.take_along_axis(
            jnp.broadcast_to(table[h : h + 1, :], index.shape), low, axis=1, mode="promise_in_bounds"
        )
        out = jnp.where(span == h, taken, out)
    return out


def unrow(row, chunks):
    return jnp.concatenate([row[:, h * LANES : (h + 1) * LANES] for h in range(chunks)], axis=0)


def rain_kernel(
    bins,
    slots,
    core_ref,
    trait_ref,
    bio_ref,
    area_ref,
    force_ref,
    source_ref,
    share_ref,
    step_ref,
    target_ref,
    water_ref,
    rate_ref,
    capacity_ref,
    out_ref,
    mate_ref,
    total_ref,
):
    step = pl.program_id(0)
    patches = area_ref.shape[0]
    chunks = step_ref.shape[0]
    rows = target_ref.shape[0]
    size = 2 * chunks + rows + 2
    peers = out_ref.shape[0] // size
    light = force_ref[0:1, :]
    light = light / (light + 0.5)

    @pl.when(step == 0)
    def _():
        total_ref[...] = jnp.zeros_like(total_ref)
        shape = (chunks, LANES)
        moves = step_ref[...]
        cell = row_iota(shape) * LANES + lane_iota(shape)
        target = jnp.where(moves > 0, cell + moves, -1).astype(F32)
        rates = [unrow(rate_ref[2 + q : 3 + q, :], chunks) for q in range(2)]
        land = target_ref[...].astype(F32)
        for j in range(peers):
            at = size * j
            out_ref[at : at + chunks, :] = target
            out_ref[at + chunks : at + 2 * chunks, :] = rates[j % 2]
            out_ref[at + 2 * chunks : at + 2 * chunks + rows, :] = land
        first = core_ref[0] == 0
        for i, (ref, at) in enumerate(((water_ref, 2), (water_ref, 0), (rate_ref, 0))):
            other = jnp.where(first, ref[at + 1 : at + 2, :], ref[at : at + 1, :])
            mate_ref[i * chunks : (i + 1) * chunks, :] = unrow(other, chunks)
        mate_ref[3 * chunks :, :] = land

    above = jnp.zeros((patches, LANES), F32)
    total = jnp.zeros((patches, LANES), F32)
    for k in reversed(range(bins)):
        leaf = bio_ref[pl.ds(k, patches, stride=bins), :] * trait_ref[0, k]
        total = total + trait_ref[1, k] * leaf * jnp.exp(-0.05 * above)
        above = above + leaf
    total_ref[...] += jnp.sum(total * light * area_ref[...], axis=0, keepdims=True)

    @pl.when(step == pl.num_programs(0) - 1)
    def _():
        shape = (peers, LANES)
        wet = force_ref[1:2, :] * force_ref[2:3, :]
        frozen = force_ref[4:5, :]
        runoff = [
            wet * (1.0 - frozen),
            wet * frozen,
            force_ref[3:4, :] * jnp.exp(-0.5 * (0.5 * total_ref[...])),
        ]
        source = by_peer(source_ref[...], peers, slots)
        share = by_peer(share_ref[...], peers, slots)
        safe = jnp.maximum(source, 0)
        section = lane_iota(shape) // slots
        value = jnp.zeros(shape, F32)
        for f in range(3):
            taken = jnp.take_along_axis(
                jnp.broadcast_to(runoff[f], shape), safe, axis=1, mode="promise_in_bounds"
            )
            value = jnp.where(section == f, taken, value)
        own = jnp.where(source >= 0, share * value, 0.0)
        mate = jnp.where(
            row_iota(shape) % 2 == 0, pltpu.roll(own, peers - 1, 0), pltpu.roll(own, 1, 0)
        )
        room = by_peer(look_up(capacity_ref[...], target_ref[...]), peers, slots)
        out_ref[pl.ds(size - 2, peers, stride=size), :] = jnp.where(section == 3, room, own)
        out_ref[pl.ds(size - 1, peers, stride=size), :] = mate


def transit_kernel(kinds, bins, trait_ref, trans_ref, bio_ref, force_ref, weight_ref, out_ref, left_ref):
    patches = trans_ref.shape[1]
    high, low = split2(trans_ref[...])
    left_ref[:, 0:patches] = high.astype(BF16)
    left_ref[:, patches : 2 * patches] = high.astype(BF16)
    left_ref[:, 2 * patches : 3 * patches] = low.astype(BF16)
    light = force_ref[0:1, :]
    light = light / (light + 0.5)
    weights = [jnp.broadcast_to(weight_ref[t : t + 1, :], (patches, LANES)) for t in range(kinds)]
    half = 0.5 * light

    def one(k, above):
        mass = bio_ref[pl.ds(k, patches, stride=bins), :]
        leaf = mass * trait_ref[0, k]
        gain = trait_ref[1, k] * leaf * jnp.exp(-0.05 * above) * half
        grown = mass * (1.0 - 0.1 * trait_ref[2, k]) + gain
        high, low = split2(grown)
        high = high.astype(BF16)
        return jnp.concatenate([high, low.astype(BF16), high], axis=0), above + leaf

    def body(i, above):
        k = bins - 1 - 2 * i
        first, above = one(k, above)
        second, above = one(k - 1, above)
        right = jnp.concatenate([first, second], axis=1)
        moved = jnp.dot(left_ref[...], right, preferred_element_type=F32)
        for j in range(2):
            part = moved[:, j * LANES : (j + 1) * LANES]
            total = part[0:patches] * weights[0]
            for t in range(1, kinds):
                total = total + part[t * patches : (t + 1) * patches] * weights[t]
            out_ref[pl.ds(k - j, patches, stride=bins), :] = total
        return above

    lax.fori_loop(0, bins // 2, body, jnp.zeros((patches, LANES), F32), unroll=4)


def river_kernel(
    slots,
    here_ref,
    arrived_ref,
    target_ref,
    mate_ref,
    water_ref,
    rate_ref,
    out_ref,
    hill_out_ref,
    room_ref,
    lo_ref,
    mask_ref,
    state_ref,
    speed_ref,
    value_ref,
    rows_left_ref,
    rows_lo_ref,
    hill_ref,
    hill_rate_ref,
    runoff_ref,
):
    chunks = state_ref.shape[1]
    rows = target_ref.shape[0]
    size = 2 * chunks + rows + 2
    peers = arrived_ref.shape[0] // size
    spans = 2 * chunks
    window = state_ref.shape[0]
    base = here_ref[0]
    core = here_ref[1]
    other = 1 - core

    def block_of(b):
        j = base + b
        return jnp.where(j >= peers, j - peers, j)

    square = (LANES, LANES)
    eye = jnp.where(row_iota(square) == lane_iota(square), 1.0, 0.0).astype(BF16)
    wide = (2 * LANES, 2 * LANES)
    ones = jnp.where(row_iota(wide) // LANES == lane_iota(wide) // LANES, 1.0, 0.0).astype(BF16)
    lane = lane_iota(square).astype(F32)

    def table(b, carry):
        j = block_of(b)
        target = arrived_ref[pl.ds(j * size, chunks), :].astype(jnp.int32)
        span = target >> 7
        low = (target & 127).astype(F32)
        for h in range(0, chunks, 2):
            diagonal = jnp.concatenate(
                [
                    jnp.broadcast_to(low[h + i : h + i + 1, :], square).astype(BF16) * eye
                    for i in range(2)
                ],
                axis=1,
            )
            column = jnp.dot(diagonal, ones, preferred_element_type=F32)
            for i in range(2):
                at = slice((h + i) * LANES, (h + i + 1) * LANES)
                mask_ref[b, h + i] = jnp.where(
                    row_iota((spans, LANES)) == span[h + i : h + i + 1, :], 1.0, 0.0
                ).astype(BF16)
                lo_ref[b, at, :] = jnp.where(
                    column[:, i * LANES : (i + 1) * LANES] == lane, 1.0, 0.0
                ).astype(BF16)
        speed_ref[b] = arrived_ref[pl.ds(j * size + chunks, chunks), :]
        return carry

    lax.fori_loop(0, window - 1, table, 0)

    fraction = 1.0 / NSUB
    half = 3 * chunks
    for which in range(2):
        if which == 0:
            target = target_ref[...]
        else:
            target = mate_ref[3 * chunks :, :].astype(jnp.int32)
        span = target >> 7
        low = target & 127
        values = [split2(from_peers(arrived_ref, rows, slots, f, size - 2 + which, size)) for f in range(3)]
        for a in range(rows):
            mask = row_iota((chunks, LANES)) == span[a : a + 1, :]
            for s in range(2):
                for f in range(3):
                    m = (s * 3 + f) * chunks
                    rows_left_ref[which, a, m : m + chunks, :] = jnp.where(
                        mask, values[f][s][a : a + 1, :], 0.0
                    ).astype(BF16)
            rows_lo_ref[which, a] = jnp.where(
                row_iota((LANES, LANES)) == low[a : a + 1, :], 1.0, 0.0
            ).astype(BF16)
        taken = nt_dot(
            jnp.concatenate([rows_left_ref[which, a] for a in range(rows)], axis=1),
            jnp.concatenate([rows_lo_ref[which, a] for a in range(rows)], axis=1),
        )
        for f in range(3):
            runoff_ref[which, f] = fraction * (
                taken[f * chunks : (f + 1) * chunks]
                + taken[half + f * chunks : half + (f + 1) * chunks]
            )

    state_ref[...] = jnp.zeros_like(state_ref)
    for q in range(2):
        hill_ref[q] = unrow(water_ref[q : q + 1, :], chunks)
        hill_rate_ref[q] = unrow(rate_ref[q : q + 1, :], chunks)
    own = jnp.where(core == 0, water_ref[2:3, :], water_ref[3:4, :])
    state_ref[core] = unrow(own, chunks)
    state_ref[other] = mate_ref[0:chunks, :]
    hill_ref[2] = mate_ref[chunks : 2 * chunks, :]
    hill_rate_ref[2] = mate_ref[2 * chunks : 3 * chunks, :]
    deep = [jnp.where(core == 0, runoff_ref[which, 2], 0.0) for which in range(2)]
    surface = [runoff_ref[0, 0], runoff_ref[0, 1], runoff_ref[1, core]]

    def block_flow(b):
        out = speed_ref[b] * state_ref[b]
        high, low = split2(out)
        value_ref[b, 0] = high
        value_ref[b, 1] = low
        pieces = []
        for h in range(chunks):
            mask = mask_ref[b, h]
            pieces.append(
                jnp.concatenate(
                    [
                        jnp.broadcast_to(value_ref[b, s, h : h + 1, :], (spans, LANES)).astype(BF16)
                        * mask
                        for s in range(2)
                    ],
                    axis=0,
                )
            )
        flow = jnp.dot(
            jnp.concatenate(pieces, axis=1), lo_ref[b], preferred_element_type=F32
        )
        return out, flow[0:spans] + flow[spans : 2 * spans]

    def advance(count):
        for b in reversed(range(count)):
            out, flow = block_flow(b)
            state_ref[b] = state_ref[b] - out + flow[0:chunks]
            state_ref[b + 1] += flow[chunks:spans]

    for phase in range(NSUB // PHASE):

        def step(t, carry):
            advance(phase * PHASE + PHASE + 1)
            gone = [hill_rate_ref[i] * hill_ref[i] for i in range(3)]
            for i in range(3):
                hill_ref[i] = hill_ref[i] - gone[i] + surface[i]
            state_ref[core] += jnp.where(core == 0, gone[0], gone[1]) + deep[0]
            state_ref[other] += gone[2] + deep[1]
            return carry

        lax.fori_loop(0, PHASE, step, 0)

    hill_out_ref[...] = hill_ref[0:2]

    shape = (peers, LANES)
    section = lane_iota(shape) // slots
    room = arrived_ref[pl.ds(size - 2, peers, stride=size), :]
    room_ref[...] = all_sections(jnp.where(section == 3, room, 0.0), slots)

    extra = -(-window * slots // LANES)
    out_size = chunks + extra
    reached = [jnp.zeros(shape, F32) for _ in range(extra)]
    for b in range(window):
        j = block_of(b)
        out_ref[pl.ds(j * out_size, chunks), :] = state_ref[b]
        index = arrived_ref[pl.ds(j * size + spans, rows), :].astype(jnp.int32)
        value = by_peer(look_up(state_ref[b], index), peers, slots)
        e, at = divmod(b * slots, LANES)
        reached[e] = jnp.where(section == at // slots, value, reached[e])
    for e in range(extra):
        out_ref[pl.ds(chunks + e, peers, stride=out_size), :] = reached[e]


def survive_kernel(
    bins,
    slots,
    window,
    here_ref,
    trait_ref,
    part_ref,
    hill_ref,
    room_ref,
    share_ref,
    source_ref,
    moved_ref,
    out_ref,
    flooded_ref,
    state_ref,
    alive_ref,
    wet_ref,
):
    peers = room_ref.shape[0]
    chunks = hill_ref.shape[1]
    size = part_ref.shape[0] // peers

    @pl.when(pl.program_id(0) == 0)
    def _():
        channel = [jnp.zeros((chunks, LANES), F32)] * 2
        for b in range(0, window, 2):
            j = here_ref[0] - b
            j = jnp.where(j < 0, j + peers, j)
            for q in range(2):
                channel[q] = channel[q] + part_ref[pl.ds((j + q) * size, chunks), :]
        for q in range(2):
            for h in range(chunks):
                at = slice(h * LANES, (h + 1) * LANES)
                state_ref[q : q + 1, at] = hill_ref[q, h : h + 1, :]
                state_ref[2 + q : 3 + q, at] = channel[q][h : h + 1, :]

        shape = (peers, LANES)
        section = lane_iota(shape) // slots
        even = row_iota(shape) % 2 == 0
        stored = jnp.zeros(shape, F32)
        for e in range(size - chunks):
            part = part_ref[pl.ds(chunks + e, peers, stride=size), :]
            part = part + jnp.where(even, pltpu.roll(part, peers - 1, 0), pltpu.roll(part, 1, 0))
            for b in range(window):
                if b * slots // LANES != e:
                    continue
                moved = pltpu.roll(part, b, 0) if b else part
                mine = (section == b * slots % LANES // slots) & (even == (b % 2 == 0))
                stored = stored + jnp.where(mine, moved, 0.0)
        stored = all_sections(stored, slots)
        wet_ref[...] = stored / (stored + room_ref[...])

        rows = share_ref.shape[0]
        value = share_ref[...] * from_peers(wet_ref, rows, slots)
        source = source_ref[...]
        total = jnp.zeros((LANES, LANES), F32)
        for a in range(rows):
            total = total + jnp.where(
                row_iota((LANES, LANES)) == source[a : a + 1, :], value[a : a + 1, :], 0.0
            )
        flooded = jnp.sum(total.T, axis=0, keepdims=True)
        flooded_ref[...] = flooded
        for k in range(bins):
            alive_ref[k : k + 1, :] = jnp.exp(-trait_ref[3, k] * flooded)

    alive = alive_ref[...]
    for p in range(moved_ref.shape[0] // bins):
        at = slice(p * bins, (p + 1) * bins)
        out_ref[at, :] = moved_ref[at, :] * alive


def shards(
    axes,
    biomass,
    patch_area,
    cohort_traits,
    cell_forcing,
    disturb_weight,
    transitions,
    land_source,
    pair_share,
    river_target,
    downstream_step,
    river_water,
    river_rates,
    capacity,
):
    patches, bins, lands = biomass.shape
    rivers = river_water.shape[1]
    peers = math.prod(lax.axis_size(a) for a in axes)
    slots = land_source.shape[0] // peers
    rows = land_source.shape[0] // LANES
    chunks = rivers // LANES
    kinds = transitions.shape[0]
    window = NSUB + 2
    place = lax.axis_index(axes).astype(jnp.int32)
    here = jnp.stack([place - place % 2, place % 2])

    bio = biomass.reshape(patches * bins, lands)
    source = land_source.reshape(rows, LANES)
    share = pair_share.reshape(rows, LANES)
    target = river_target.reshape(rows, LANES)
    step = downstream_step.reshape(chunks, LANES)

    def exchange(message, size):
        inner = math.gcd(size, 8)
        message = message.reshape(peers, size // inner, inner, LANES)
        arrived = lax.all_to_all(message, axes, split_axis=0, concat_axis=0, tiled=True)
        return arrived.reshape(peers * size, LANES)

    size = 2 * chunks + rows + 2
    tile = 16
    whole = lambda *shape: pl.BlockSpec(shape, lambda i: (0,) * len(shape))
    message, mate = pl.pallas_call(
        functools.partial(rain_kernel, bins, slots),
        grid=(patches // tile,),
        out_shape=(
            jax.ShapeDtypeStruct((peers * size, LANES), F32),
            jax.ShapeDtypeStruct((3 * chunks + rows, LANES), F32),
        ),
        in_specs=[
            SMEM,
            SMEM,
            pl.BlockSpec((tile * bins, LANES), lambda i: (i, 0)),
            pl.BlockSpec((tile, LANES), lambda i: (i, 0)),
            whole(5, LANES),
            whole(rows, LANES),
            whole(rows, LANES),
            whole(chunks, LANES),
            whole(rows, LANES),
            whole(4, rivers),
            whole(4, rivers),
            whole(chunks, LANES),
        ],
        out_specs=(whole(peers * size, LANES), whole(3 * chunks + rows, LANES)),
        scratch_shapes=[pltpu.VMEM((1, LANES), F32)],
        name="rain",
    )(
        here[1:2],
        cohort_traits,
        bio,
        patch_area,
        cell_forcing,
        source,
        share,
        step,
        target,
        river_water,
        river_rates,
        capacity.reshape(chunks, LANES),
    )
    arrived = exchange(message, size)
    mate = lax.ppermute(mate, axes, [(i, i + 1 - 2 * (i % 2)) for i in range(peers)])

    moved = pl.pallas_call(
        functools.partial(transit_kernel, kinds, bins),
        out_shape=jax.ShapeDtypeStruct((patches * bins, LANES), F32),
        in_specs=[SMEM, VMEM, VMEM, VMEM, VMEM],
        out_specs=VMEM,
        scratch_shapes=[pltpu.VMEM((kinds * patches, 3 * patches), BF16)],
        name="transit",
    )(cohort_traits, transitions.reshape(kinds * patches, patches), bio, cell_forcing, disturb_weight)

    spans = 2 * chunks
    out_size = chunks - (-window * slots // LANES)
    parts, hill, room = pl.pallas_call(
        functools.partial(river_kernel, slots),
        out_shape=(
            jax.ShapeDtypeStruct((peers * out_size, LANES), F32),
            jax.ShapeDtypeStruct((2, chunks, LANES), F32),
            jax.ShapeDtypeStruct((peers, LANES), F32),
        ),
        in_specs=[SMEM] + [VMEM] * 5,
        out_specs=(VMEM, VMEM, VMEM),
        scratch_shapes=[
            pltpu.VMEM((window - 1, rivers, LANES), BF16),
            pltpu.VMEM((window - 1, chunks, spans, LANES), BF16),
            pltpu.VMEM((window, chunks, LANES), F32),
            pltpu.VMEM((window - 1, chunks, LANES), F32),
            pltpu.VMEM((window - 1, 2, chunks, LANES), F32),
            pltpu.VMEM((2, rows, 6 * chunks, LANES), BF16),
            pltpu.VMEM((2, rows, LANES, LANES), BF16),
            pltpu.VMEM((3, chunks, LANES), F32),
            pltpu.VMEM((3, chunks, LANES), F32),
            pltpu.VMEM((2, 3, chunks, LANES), F32),
        ],
        name="river",
    )(here, arrived, target, mate, river_water, river_rates)
    parts = exchange(parts, out_size)

    tile = 12
    new_biomass, flooded, river_state = pl.pallas_call(
        functools.partial(survive_kernel, bins, slots, window),
        grid=(patches // tile,),
        out_shape=(
            jax.ShapeDtypeStruct((patches * bins, LANES), F32),
            jax.ShapeDtypeStruct((1, LANES), F32),
            jax.ShapeDtypeStruct((4, rivers), F32),
        ),
        in_specs=[
            SMEM,
            SMEM,
            whole(peers * out_size, LANES),
            whole(2, chunks, LANES),
            whole(peers, LANES),
            whole(rows, LANES),
            whole(rows, LANES),
            pl.BlockSpec((tile * bins, LANES), lambda i: (i, 0)),
        ],
        out_specs=(
            pl.BlockSpec((tile * bins, LANES), lambda i: (i, 0)),
            whole(1, LANES),
            whole(4, rivers),
        ),
        scratch_shapes=[pltpu.VMEM((bins, LANES), F32), pltpu.VMEM((peers, LANES), F32)],
        name="survive",
    )(here, cohort_traits, parts, hill, room, share, source, moved)
    return (new_biomass.reshape(patches, bins, lands), flooded.reshape(lands), river_state)


def solution(mesh):
    axes = tuple(mesh.axis_names)
    split = P(axes)
    split1 = P(None, axes)

    def body(*args):
        return shards(axes, *args)

    return jax.shard_map(
        body,
        mesh=mesh,
        in_specs=(
            P(None, None, axes),
            split1,
            P(),
            split1,
            split1,
            P(),
            split,
            split,
            split,
            split,
            split1,
            split1,
            split,
        ),
        out_specs=(P(None, None, axes), split, split1),
        check_vma=False,
    )
```

```python
import functools
import math

import jax
import jax.numpy as jnp
from jax import lax
from jax.experimental import pallas as pl
from jax.experimental.pallas import tpu as pltpu
from jax.sharding import PartitionSpec as P


NSUB = 12
LANES = 128
F32 = jnp.float32
BF16 = jnp.bfloat16

VMEM = pl.BlockSpec(memory_space=pltpu.VMEM)
ANY = pl.BlockSpec(memory_space=pl.ANY)
SMEM = pl.BlockSpec(memory_space=pltpu.SMEM)


def on_chip(value):
    return pltpu.with_memory_space_constraint(value, pltpu.VMEM)


def lane_iota(shape):
    return lax.broadcasted_iota(jnp.int32, shape, len(shape) - 1)


def row_iota(shape):
    return lax.broadcasted_iota(jnp.int32, shape, 0)


def nt_dot(a, b):
    return lax.dot_general(a, b, (((1,), (1,)), ((), ())), preferred_element_type=F32)


def split2(x):
    high = x.astype(BF16).astype(F32)
    return high, x - high


def by_peer(value, peers, slots):
    rows = value.shape[0]
    per = peers // rows
    spread = jnp.concatenate(
        [jnp.broadcast_to(value[a : a + 1, :], (per, LANES)) for a in range(rows)], axis=0
    )
    shape = (peers, LANES)
    index = (row_iota(shape) % per) * slots + lane_iota(shape) % slots
    return jnp.take_along_axis(spread, index, axis=1, mode="promise_in_bounds")


def from_peers(ref, rows, slots, feature=None, which=0, count=1):
    peers = ref.shape[0] // count
    per = peers // rows
    section = lane_iota((rows, LANES)) // slots
    out = jnp.zeros((rows, LANES), F32)
    for b in range(per):
        part = ref[pl.ds(b * count + which, rows, stride=per * count), :]
        if feature is not None:
            shift = ((b - feature) * slots) % LANES
            if shift:
                part = pltpu.roll(part, shift, 1)
        out = jnp.where(section == b, part, out)
    return out


def all_sections(value, slots):
    shift = slots
    while shift < LANES:
        value = value + pltpu.roll(value, shift, 1)
        shift *= 2
    return value


def look_up(table, index):
    span = index >> 7
    low = index & 127
    out = jnp.zeros(index.shape, F32)
    for h in range(table.shape[0]):
        taken = jnp.take_along_axis(
            jnp.broadcast_to(table[h : h + 1, :], index.shape), low, axis=1, mode="promise_in_bounds"
        )
        out = jnp.where(span == h, taken, out)
    return out


def unrow(row, chunks):
    return jnp.concatenate([row[:, h * LANES : (h + 1) * LANES] for h in range(chunks)], axis=0)


def rain_kernel(
    bins,
    slots,
    core_ref,
    trait_ref,
    bio_ref,
    area_ref,
    force_ref,
    source_ref,
    share_ref,
    step_ref,
    target_ref,
    water_ref,
    rate_ref,
    capacity_ref,
    out_ref,
    mate_ref,
    total_ref,
):
    step = pl.program_id(0)
    patches = area_ref.shape[0]
    chunks = step_ref.shape[0]
    rows = target_ref.shape[0]
    size = 2 * chunks + rows + 2
    peers = out_ref.shape[0] // size
    light = force_ref[0:1, :]
    light = light / (light + 0.5)

    @pl.when(step == 0)
    def _():
        total_ref[...] = jnp.zeros_like(total_ref)
        shape = (chunks, LANES)
        moves = step_ref[...]
        cell = row_iota(shape) * LANES + lane_iota(shape)
        target = jnp.where(moves > 0, cell + moves, -1).astype(F32)
        rates = [unrow(rate_ref[2 + q : 3 + q, :], chunks) for q in range(2)]
        land = target_ref[...].astype(F32)
        for j in range(peers):
            at = size * j
            out_ref[at : at + chunks, :] = target
            out_ref[at + chunks : at + 2 * chunks, :] = rates[j % 2]
            out_ref[at + 2 * chunks : at + 2 * chunks + rows, :] = land
        first = core_ref[0] == 0
        for i, (ref, at) in enumerate(((water_ref, 2), (water_ref, 0), (rate_ref, 0))):
            other = jnp.where(first, ref[at + 1 : at + 2, :], ref[at : at + 1, :])
            mate_ref[i * chunks : (i + 1) * chunks, :] = unrow(other, chunks)
        mate_ref[3 * chunks :, :] = land

    above = jnp.zeros((patches, LANES), F32)
    total = jnp.zeros((patches, LANES), F32)
    for k in reversed(range(bins)):
        leaf = bio_ref[pl.ds(k, patches, stride=bins), :] * trait_ref[0, k]
        total = total + trait_ref[1, k] * leaf * jnp.exp(-0.05 * above)
        above = above + leaf
    total_ref[...] += jnp.sum(total * light * area_ref[...], axis=0, keepdims=True)

    @pl.when(step == pl.num_programs(0) - 1)
    def _():
        shape = (peers, LANES)
        wet = force_ref[1:2, :] * force_ref[2:3, :]
        frozen = force_ref[4:5, :]
        runoff = [
            wet * (1.0 - frozen),
            wet * frozen,
            force_ref[3:4, :] * jnp.exp(-0.5 * (0.5 * total_ref[...])),
        ]
        source = by_peer(source_ref[...], peers, slots)
        share = by_peer(share_ref[...], peers, slots)
        safe = jnp.maximum(source, 0)
        section = lane_iota(shape) // slots
        value = jnp.zeros(shape, F32)
        for f in range(3):
            taken = jnp.take_along_axis(
                jnp.broadcast_to(runoff[f], shape), safe, axis=1, mode="promise_in_bounds"
            )
            value = jnp.where(section == f, taken, value)
        own = jnp.where(source >= 0, share * value, 0.0)
        mate = jnp.where(
            row_iota(shape) % 2 == 0, pltpu.roll(own, peers - 1, 0), pltpu.roll(own, 1, 0)
        )
        room = by_peer(look_up(capacity_ref[...], target_ref[...]), peers, slots)
        out_ref[pl.ds(size - 2, peers, stride=size), :] = jnp.where(section == 3, room, own)
        out_ref[pl.ds(size - 1, peers, stride=size), :] = mate


def transit_kernel(kinds, bins, trait_ref, trans_ref, bio_ref, force_ref, weight_ref, out_ref, left_ref):
    patches = trans_ref.shape[1]
    high, low = split2(trans_ref[...])
    left_ref[:, 0:patches] = high.astype(BF16)
    left_ref[:, patches : 2 * patches] = high.astype(BF16)
    left_ref[:, 2 * patches : 3 * patches] = low.astype(BF16)
    light = force_ref[0:1, :]
    light = light / (light + 0.5)
    weights = [jnp.broadcast_to(weight_ref[t : t + 1, :], (patches, LANES)) for t in range(kinds)]
    half = 0.5 * light

    def one(k, above):
        mass = bio_ref[pl.ds(k, patches, stride=bins), :]
        leaf = mass * trait_ref[0, k]
        gain = trait_ref[1, k] * leaf * jnp.exp(-0.05 * above) * half
        grown = mass * (1.0 - 0.1 * trait_ref[2, k]) + gain
        high, low = split2(grown)
        high = high.astype(BF16)
        return jnp.concatenate([high, low.astype(BF16), high], axis=0), above + leaf

    def body(i, above):
        k = bins - 1 - 2 * i
        first, above = one(k, above)
        second, above = one(k - 1, above)
        right = jnp.concatenate([first, second], axis=1)
        moved = jnp.dot(left_ref[...], right, preferred_element_type=F32)
        for j in range(2):
            part = moved[:, j * LANES : (j + 1) * LANES]
            total = part[0:patches] * weights[0]
            for t in range(1, kinds):
                total = total + part[t * patches : (t + 1) * patches] * weights[t]
            out_ref[pl.ds(k - j, patches, stride=bins), :] = total
        return above

    lax.fori_loop(0, bins // 2, body, jnp.zeros((patches, LANES), F32), unroll=4)


def river_kernel(
    slots,
    here_ref,
    arrived_ref,
    target_ref,
    mate_ref,
    water_ref,
    rate_ref,
    out_ref,
    hill_out_ref,
    room_ref,
    lo_refs,
    mask_refs,
    speed_refs,
    state_ref,
    value_ref,
    rows_left_ref,
    rows_lo_ref,
    hill_ref,
    hill_rate_ref,
    runoff_ref,
):
    chunks = state_ref.shape[1]
    rows = target_ref.shape[0]
    size = 2 * chunks + rows + 2
    peers = arrived_ref.shape[0] // size
    spans = 2 * chunks
    window = NSUB + 2
    base = here_ref[0]
    core = here_ref[1]
    other = 1 - core

    def block_of(b):
        j = base + b
        return jnp.where(j >= peers, j - peers, j)

    square = (LANES, LANES)
    lane = lane_iota(square).astype(F32)
    eye = jnp.where(row_iota(square) == lane_iota(square), 1.0, 0.0).astype(BF16)
    wide = (2 * LANES, 2 * LANES)
    ones = jnp.where(row_iota(wide) // LANES == lane_iota(wide) // LANES, 1.0, 0.0).astype(BF16)

    def table(pair, at):
        j = block_of(2 * pair + at)
        target = arrived_ref[pl.ds(j * size, chunks), :].astype(jnp.int32)
        span = target >> 7
        low = (target & 127).astype(F32)
        half = chunks // 2
        diagonal = jnp.concatenate(
            [
                jnp.concatenate(
                    [
                        jnp.broadcast_to(low[h + i * half : h + i * half + 1, :], square).astype(BF16)
                        * eye
                        for h in range(half)
                    ],
                    axis=0,
                )
                for i in range(2)
            ],
            axis=1,
        )
        columns = jnp.dot(diagonal, ones, preferred_element_type=F32)
        for h in range(chunks):
            i, k = divmod(h, half)
            column = columns[k * LANES : (k + 1) * LANES, i * LANES : (i + 1) * LANES]
            mask_refs[pair][at, h] = jnp.where(
                row_iota((spans, LANES)) == span[h : h + 1, :], 1.0, 0.0
            ).astype(BF16)
            lo_refs[pair][at, h * LANES : (h + 1) * LANES, :] = jnp.where(
                column == lane, 1.0, 0.0
            ).astype(BF16)
        speed_refs[pair][at] = arrived_ref[pl.ds(j * size + chunks, chunks), :]

    table(0, 0)
    table(0, 1)

    fraction = 1.0 / NSUB
    half = 3 * chunks
    for which in range(2):
        if which == 0:
            target = target_ref[...]
        else:
            target = mate_ref[3 * chunks :, :].astype(jnp.int32)
        span = target >> 7
        low = target & 127
        values = [split2(from_peers(arrived_ref, rows, slots, f, size - 2 + which, size)) for f in range(3)]
        for a in range(rows):
            mask = row_iota((chunks, LANES)) == span[a : a + 1, :]
            for s in range(2):
                for f in range(3):
                    m = (s * 3 + f) * chunks
                    rows_left_ref[which, a, m : m + chunks, :] = jnp.where(
                        mask, values[f][s][a : a + 1, :], 0.0
                    ).astype(BF16)
            rows_lo_ref[which, a] = jnp.where(
                row_iota((LANES, LANES)) == low[a : a + 1, :], 1.0, 0.0
            ).astype(BF16)
        taken = nt_dot(
            jnp.concatenate([rows_left_ref[which, a] for a in range(rows)], axis=1),
            jnp.concatenate([rows_lo_ref[which, a] for a in range(rows)], axis=1),
        )
        for f in range(3):
            runoff_ref[which, f] = fraction * (
                taken[f * chunks : (f + 1) * chunks]
                + taken[half + f * chunks : half + (f + 1) * chunks]
            )

    state_ref[...] = jnp.zeros_like(state_ref)
    for q in range(2):
        hill_ref[q] = unrow(water_ref[q : q + 1, :], chunks)
        hill_rate_ref[q] = unrow(rate_ref[q : q + 1, :], chunks)
    own = jnp.where(core == 0, water_ref[2:3, :], water_ref[3:4, :])
    state_ref[core] = unrow(own, chunks)
    state_ref[other] = mate_ref[0:chunks, :]
    hill_ref[2] = mate_ref[chunks : 2 * chunks, :]
    hill_rate_ref[2] = mate_ref[2 * chunks : 3 * chunks, :]
    deep = [jnp.where(core == 0, runoff_ref[which, 2], 0.0) for which in range(2)]
    surface = [runoff_ref[0, 0], runoff_ref[0, 1], runoff_ref[1, core]]

    def pair_flow(pair):
        outs = []
        for i in range(2):
            out = speed_refs[pair][i] * state_ref[2 * pair + i]
            high, low = split2(out)
            value_ref[pair, 2 * i] = high
            value_ref[pair, 2 * i + 1] = low
            outs.append(out)
        pieces = []
        for h in range(chunks):
            masks = [mask_refs[pair][i, h] for i in range(2)]
            pieces.append(
                jnp.concatenate(
                    [
                        jnp.broadcast_to(value_ref[pair, m, h : h + 1, :], (spans, LANES)).astype(BF16)
                        * masks[m // 2]
                        for m in range(4)
                    ],
                    axis=0,
                )
            )
        flow = jnp.dot(
            jnp.concatenate(pieces, axis=1),
            jnp.concatenate([lo_refs[pair][0], lo_refs[pair][1]], axis=1),
            preferred_element_type=F32,
        )
        flows = []
        for i in range(2):
            part = flow[2 * i * spans : 2 * (i + 1) * spans, i * LANES : (i + 1) * LANES]
            flows.append(part[0:spans] + part[spans:])
        return outs, flows

    def advance(pairs):
        for pair in reversed(range(pairs)):
            outs, flows = pair_flow(pair)
            b = 2 * pair
            state_ref[b + 2] += flows[1][chunks:]
            state_ref[b + 1] = state_ref[b + 1] - outs[1] + flows[1][:chunks] + flows[0][chunks:]
            state_ref[b] = state_ref[b] - outs[0] + flows[0][:chunks]
        gone = [hill_rate_ref[i] * hill_ref[i] for i in range(3)]
        for i in range(3):
            hill_ref[i] = hill_ref[i] - gone[i] + surface[i]
        state_ref[core] += jnp.where(core == 0, gone[0], gone[1]) + deep[0]
        state_ref[other] += gone[2] + deep[1]

    table(1, 0)
    table(1, 1)
    advance(1)
    for pairs in range(2, NSUB // 2 + 1):

        def step(i, carry):
            table(pairs, i)
            advance(pairs)
            return carry

        lax.fori_loop(0, 2, step, 0)
    advance(NSUB // 2 + 1)

    hill_out_ref[...] = hill_ref[0:2]

    shape = (peers, LANES)
    section = lane_iota(shape) // slots
    room = arrived_ref[pl.ds(size - 2, peers, stride=size), :]
    room_ref[...] = all_sections(jnp.where(section == 3, room, 0.0), slots)

    extra = -(-window * slots // LANES)
    out_size = chunks + extra
    reached = [jnp.zeros(shape, F32) for _ in range(extra)]
    for b in range(window):
        j = block_of(b)
        out_ref[pl.ds(j * out_size, chunks), :] = state_ref[b]
        index = arrived_ref[pl.ds(j * size + spans, rows), :].astype(jnp.int32)
        value = by_peer(look_up(state_ref[b], index), peers, slots)
        e, at = divmod(b * slots, LANES)
        reached[e] = jnp.where(section == at // slots, value, reached[e])
    for e in range(extra):
        out_ref[pl.ds(chunks + e, peers, stride=out_size), :] = reached[e]


def survive_kernel(
    bins,
    slots,
    window,
    here_ref,
    trait_ref,
    part_ref,
    hill_ref,
    room_ref,
    share_ref,
    source_ref,
    moved_ref,
    out_ref,
    flooded_ref,
    state_ref,
    alive_ref,
    wet_ref,
):
    peers = room_ref.shape[0]
    chunks = hill_ref.shape[1]
    size = part_ref.shape[0] // peers

    @pl.when(pl.program_id(0) == 0)
    def _():
        channel = [jnp.zeros((chunks, LANES), F32)] * 2
        for b in range(0, window, 2):
            j = here_ref[0] - b
            j = jnp.where(j < 0, j + peers, j)
            for q in range(2):
                channel[q] = channel[q] + part_ref[pl.ds((j + q) * size, chunks), :]
        for q in range(2):
            for h in range(chunks):
                at = slice(h * LANES, (h + 1) * LANES)
                state_ref[q : q + 1, at] = hill_ref[q, h : h + 1, :]
                state_ref[2 + q : 3 + q, at] = channel[q][h : h + 1, :]

        shape = (peers, LANES)
        section = lane_iota(shape) // slots
        even = row_iota(shape) % 2 == 0
        stored = jnp.zeros(shape, F32)
        for e in range(size - chunks):
            part = part_ref[pl.ds(chunks + e, peers, stride=size), :]
            part = part + jnp.where(even, pltpu.roll(part, peers - 1, 0), pltpu.roll(part, 1, 0))
            for b in range(window):
                if b * slots // LANES != e:
                    continue
                moved = pltpu.roll(part, b, 0) if b else part
                mine = (section == b * slots % LANES // slots) & (even == (b % 2 == 0))
                stored = stored + jnp.where(mine, moved, 0.0)
        stored = all_sections(stored, slots)
        wet_ref[...] = stored / (stored + room_ref[...])

        rows = share_ref.shape[0]
        value = share_ref[...] * from_peers(wet_ref, rows, slots)
        source = source_ref[...]
        total = jnp.zeros((LANES, LANES), F32)
        for a in range(rows):
            total = total + jnp.where(
                row_iota((LANES, LANES)) == source[a : a + 1, :], value[a : a + 1, :], 0.0
            )
        flooded = jnp.sum(total.T, axis=0, keepdims=True)
        flooded_ref[...] = flooded
        for k in range(bins):
            alive_ref[k : k + 1, :] = jnp.exp(-trait_ref[3, k] * flooded)

    alive = alive_ref[...]
    base = pl.program_id(0) * out_ref.shape[0]
    for p in range(out_ref.shape[0] // bins):
        at = pl.ds(pl.multiple_of(base + p * bins, bins), bins)
        out_ref[p * bins : (p + 1) * bins, :] = moved_ref[at, :] * alive


def shards(
    axes,
    biomass,
    patch_area,
    cohort_traits,
    cell_forcing,
    disturb_weight,
    transitions,
    land_source,
    pair_share,
    river_target,
    downstream_step,
    river_water,
    river_rates,
    capacity,
):
    patches, bins, lands = biomass.shape
    rivers = river_water.shape[1]
    peers = math.prod(lax.axis_size(a) for a in axes)
    slots = land_source.shape[0] // peers
    rows = land_source.shape[0] // LANES
    chunks = rivers // LANES
    kinds = transitions.shape[0]
    window = NSUB + 2
    place = lax.axis_index(axes).astype(jnp.int32)
    here = jnp.stack([place - place % 2, place % 2])

    bio = biomass.reshape(patches * bins, lands)
    source = land_source.reshape(rows, LANES)
    share = pair_share.reshape(rows, LANES)
    target = river_target.reshape(rows, LANES)
    step = downstream_step.reshape(chunks, LANES)

    def exchange(message, size):
        inner = math.gcd(size, 8)
        message = message.reshape(peers, size // inner, inner, LANES)
        arrived = lax.all_to_all(message, axes, split_axis=0, concat_axis=0, tiled=True)
        return on_chip(arrived.reshape(peers * size, LANES))

    size = 2 * chunks + rows + 2
    tile = 16
    whole = lambda *shape: pl.BlockSpec(shape, lambda i: (0,) * len(shape))
    message, mate = pl.pallas_call(
        functools.partial(rain_kernel, bins, slots),
        grid=(patches // tile,),
        out_shape=(
            pltpu.VMEM((peers * size, LANES), F32),
            pltpu.VMEM((3 * chunks + rows, LANES), F32),
        ),
        in_specs=[
            SMEM,
            SMEM,
            pl.BlockSpec((tile * bins, LANES), lambda i: (i, 0)),
            pl.BlockSpec((tile, LANES), lambda i: (i, 0)),
            whole(5, LANES),
            whole(rows, LANES),
            whole(rows, LANES),
            whole(chunks, LANES),
            whole(rows, LANES),
            whole(4, rivers),
            whole(4, rivers),
            whole(chunks, LANES),
        ],
        out_specs=(whole(peers * size, LANES), whole(3 * chunks + rows, LANES)),
        scratch_shapes=[pltpu.VMEM((1, LANES), F32)],
        compiler_params=pltpu.CompilerParams(vmem_limit_bytes=16 << 20),
        name="rain",
    )(
        here[1:2],
        cohort_traits,
        bio,
        patch_area,
        cell_forcing,
        source,
        share,
        step,
        target,
        river_water,
        river_rates,
        capacity.reshape(chunks, LANES),
    )
    arrived = exchange(message, size)
    mate = on_chip(lax.ppermute(mate, axes, [(i, i + 1 - 2 * (i % 2)) for i in range(peers)]))

    moved = pl.pallas_call(
        functools.partial(transit_kernel, kinds, bins),
        out_shape=pltpu.VMEM((patches * bins, LANES), F32),
        in_specs=[SMEM, VMEM, VMEM, VMEM, VMEM],
        out_specs=VMEM,
        scratch_shapes=[pltpu.VMEM((kinds * patches, 3 * patches), BF16)],
        compiler_params=pltpu.CompilerParams(vmem_limit_bytes=16 << 20),
        name="transit",
    )(cohort_traits, transitions.reshape(kinds * patches, patches), bio, cell_forcing, disturb_weight)

    spans = 2 * chunks
    out_size = chunks - (-window * slots // LANES)
    parts, hill, room = pl.pallas_call(
        functools.partial(river_kernel, slots),
        out_shape=(
            pltpu.VMEM((peers * out_size, LANES), F32),
            pltpu.VMEM((2, chunks, LANES), F32),
            pltpu.VMEM((peers, LANES), F32),
        ),
        in_specs=[SMEM] + [VMEM] * 5,
        out_specs=(VMEM, VMEM, VMEM),
        scratch_shapes=[
            [pltpu.VMEM((2, rivers, LANES), BF16)] * (window // 2),
            [pltpu.VMEM((2, chunks, spans, LANES), BF16)] * (window // 2),
            [pltpu.VMEM((2, chunks, LANES), F32)] * (window // 2),
            pltpu.VMEM((window + 1, chunks, LANES), F32),
            pltpu.VMEM((window // 2, 4, chunks, LANES), F32),
            pltpu.VMEM((2, rows, 6 * chunks, LANES), BF16),
            pltpu.VMEM((2, rows, LANES, LANES), BF16),
            pltpu.VMEM((3, chunks, LANES), F32),
            pltpu.VMEM((3, chunks, LANES), F32),
            pltpu.VMEM((2, 3, chunks, LANES), F32),
        ],
        compiler_params=pltpu.CompilerParams(vmem_limit_bytes=32 << 20),
        name="river",
    )(here, arrived, target, mate, river_water, river_rates)
    parts = exchange(parts, out_size)

    tile = 12
    new_biomass, flooded, river_state = pl.pallas_call(
        functools.partial(survive_kernel, bins, slots, window),
        grid=(patches // tile,),
        out_shape=(
            jax.ShapeDtypeStruct((patches * bins, LANES), F32),
            jax.ShapeDtypeStruct((1, LANES), F32),
            jax.ShapeDtypeStruct((4, rivers), F32),
        ),
        in_specs=[
            SMEM,
            SMEM,
            VMEM,
            VMEM,
            VMEM,
            whole(rows, LANES),
            whole(rows, LANES),
            VMEM,
        ],
        out_specs=(
            pl.BlockSpec((tile * bins, LANES), lambda i: (i, 0)),
            whole(1, LANES),
            whole(4, rivers),
        ),
        scratch_shapes=[pltpu.VMEM((bins, LANES), F32), pltpu.VMEM((peers, LANES), F32)],
        compiler_params=pltpu.CompilerParams(vmem_limit_bytes=16 << 20),
        name="survive",
    )(here, cohort_traits, parts, on_chip(hill), on_chip(room), share, source, on_chip(moved))
    return (new_biomass.reshape(patches, bins, lands), flooded.reshape(lands), river_state)


def solution(mesh):
    axes = tuple(mesh.axis_names)
    split = P(axes)
    split1 = P(None, axes)

    def body(*args):
        return shards(axes, *args)

    return jax.shard_map(
        body,
        mesh=mesh,
        in_specs=(
            P(None, None, axes),
            split1,
            P(),
            split1,
            split1,
            P(),
            split,
            split,
            split,
            split,
            split1,
            split1,
            split,
        ),
        out_specs=(P(None, None, axes), split, split1),
        check_vma=False,
    )
```

```python
import functools
import math

import jax
import jax.numpy as jnp
from jax import lax
from jax.experimental import pallas as pl
from jax.experimental.pallas import tpu as pltpu
from jax.sharding import PartitionSpec as P


NSUB = 12
LANES = 128
F32 = jnp.float32
BF16 = jnp.bfloat16

VMEM = pl.BlockSpec(memory_space=pltpu.VMEM)
ANY = pl.BlockSpec(memory_space=pl.ANY)
SMEM = pl.BlockSpec(memory_space=pltpu.SMEM)


def on_chip(value):
    return pltpu.with_memory_space_constraint(value, pltpu.VMEM)


def lane_iota(shape):
    return lax.broadcasted_iota(jnp.int32, shape, len(shape) - 1)


def row_iota(shape):
    return lax.broadcasted_iota(jnp.int32, shape, 0)


def nt_dot(a, b):
    return lax.dot_general(a, b, (((1,), (1,)), ((), ())), preferred_element_type=F32)


def split2(x):
    high = x.astype(BF16).astype(F32)
    return high, x - high


def by_peer(value, peers, slots):
    rows = value.shape[0]
    per = peers // rows
    spread = jnp.concatenate(
        [jnp.broadcast_to(value[a : a + 1, :], (per, LANES)) for a in range(rows)], axis=0
    )
    shape = (peers, LANES)
    index = (row_iota(shape) % per) * slots + lane_iota(shape) % slots
    return jnp.take_along_axis(spread, index, axis=1, mode="promise_in_bounds")


def from_peers(ref, rows, slots, feature=None, which=0, count=1):
    peers = ref.shape[0] // count
    per = peers // rows
    section = lane_iota((rows, LANES)) // slots
    out = jnp.zeros((rows, LANES), F32)
    for b in range(per):
        part = ref[pl.ds(b * count + which, rows, stride=per * count), :]
        if feature is not None:
            shift = ((b - feature) * slots) % LANES
            if shift:
                part = pltpu.roll(part, shift, 1)
        out = jnp.where(section == b, part, out)
    return out


def all_sections(value, slots):
    shift = slots
    while shift < LANES:
        value = value + pltpu.roll(value, shift, 1)
        shift *= 2
    return value


def look_up(table, index):
    span = index >> 7
    low = index & 127
    out = jnp.zeros(index.shape, F32)
    for h in range(table.shape[0]):
        taken = jnp.take_along_axis(
            jnp.broadcast_to(table[h : h + 1, :], index.shape), low, axis=1, mode="promise_in_bounds"
        )
        out = jnp.where(span == h, taken, out)
    return out


def unrow(row, chunks):
    return jnp.concatenate([row[:, h * LANES : (h + 1) * LANES] for h in range(chunks)], axis=0)


def rain_kernel(
    bins,
    slots,
    core_ref,
    trait_ref,
    bio_ref,
    area_ref,
    force_ref,
    source_ref,
    share_ref,
    step_ref,
    target_ref,
    water_ref,
    rate_ref,
    capacity_ref,
    out_ref,
    mate_ref,
    total_ref,
    trait_rows_ref,
):
    step = pl.program_id(0)
    patches = area_ref.shape[0]
    chunks = step_ref.shape[0]
    rows = target_ref.shape[0]
    size = 2 * chunks + rows + 2
    peers = out_ref.shape[0] // size
    light = force_ref[0:1, :]
    light = light / (light + 0.5)

    @pl.when(step == 0)
    def _():
        total_ref[...] = jnp.zeros_like(total_ref)
        for i in range(2):
            for k in range(bins):
                trait_rows_ref[i, k : k + 1, :] = jnp.full((1, LANES), trait_ref[i, k])
        shape = (chunks, LANES)
        moves = step_ref[...]
        cell = row_iota(shape) * LANES + lane_iota(shape)
        target = jnp.where(moves > 0, cell + moves, -1).astype(F32)
        rates = [unrow(rate_ref[2 + q : 3 + q, :], chunks) for q in range(2)]
        land = target_ref[...].astype(F32)
        for j in range(peers):
            at = size * j
            out_ref[at : at + chunks, :] = target
            out_ref[at + chunks : at + 2 * chunks, :] = rates[j % 2]
            out_ref[at + 2 * chunks : at + 2 * chunks + rows, :] = land
        first = core_ref[0] == 0
        for i, (ref, at) in enumerate(((water_ref, 2), (water_ref, 0), (rate_ref, 0))):
            other = jnp.where(first, ref[at + 1 : at + 2, :], ref[at : at + 1, :])
            mate_ref[i * chunks : (i + 1) * chunks, :] = unrow(other, chunks)
        mate_ref[3 * chunks :, :] = land

    pair = (bins, bins)
    taller = jnp.where(lane_iota(pair) > row_iota(pair), 1.0, 0.0).astype(BF16)
    total = jnp.zeros((8, LANES), F32)
    for p in range(patches):
        leaf = bio_ref[p * bins : (p + 1) * bins, :] * trait_rows_ref[0]
        high, low = split2(leaf)
        above = jnp.dot(
            taller,
            jnp.concatenate([high.astype(BF16), low.astype(BF16)], axis=1),
            preferred_element_type=F32,
        )
        above = above[:, :LANES] + above[:, LANES:]
        gain = leaf * trait_rows_ref[1] * jnp.exp(-0.05 * above)
        part = gain[0:8]
        for k in range(8, bins, 8):
            part = part + gain[k : k + 8]
        total = total + part * area_ref[p : p + 1, :]
    total_ref[...] += jnp.sum(total, axis=0, keepdims=True) * light

    @pl.when(step == pl.num_programs(0) - 1)
    def _():
        shape = (peers, LANES)
        wet = force_ref[1:2, :] * force_ref[2:3, :]
        frozen = force_ref[4:5, :]
        runoff = [
            wet * (1.0 - frozen),
            wet * frozen,
            force_ref[3:4, :] * jnp.exp(-0.5 * (0.5 * total_ref[...])),
        ]
        source = by_peer(source_ref[...], peers, slots)
        share = by_peer(share_ref[...], peers, slots)
        safe = jnp.maximum(source, 0)
        section = lane_iota(shape) // slots
        value = jnp.zeros(shape, F32)
        for f in range(3):
            taken = jnp.take_along_axis(
                jnp.broadcast_to(runoff[f], shape), safe, axis=1, mode="promise_in_bounds"
            )
            value = jnp.where(section == f, taken, value)
        own = jnp.where(source >= 0, share * value, 0.0)
        mate = jnp.where(
            row_iota(shape) % 2 == 0, pltpu.roll(own, peers - 1, 0), pltpu.roll(own, 1, 0)
        )
        room = by_peer(look_up(capacity_ref[...], target_ref[...]), peers, slots)
        out_ref[pl.ds(size - 2, peers, stride=size), :] = jnp.where(section == 3, room, own)
        out_ref[pl.ds(size - 1, peers, stride=size), :] = mate


def transit_kernel(kinds, bins, trait_ref, trans_ref, bio_ref, force_ref, weight_ref, out_ref, left_ref):
    patches = trans_ref.shape[1]
    high, low = split2(trans_ref[...])
    left_ref[:, 0:patches] = high.astype(BF16)
    left_ref[:, patches : 2 * patches] = high.astype(BF16)
    left_ref[:, 2 * patches : 3 * patches] = low.astype(BF16)
    light = force_ref[0:1, :]
    light = light / (light + 0.5)
    weights = [jnp.broadcast_to(weight_ref[t : t + 1, :], (patches, LANES)) for t in range(kinds)]
    half = 0.5 * light

    def one(k, above):
        mass = bio_ref[pl.ds(k, patches, stride=bins), :]
        leaf = mass * trait_ref[0, k]
        gain = trait_ref[1, k] * leaf * jnp.exp(-0.05 * above) * half
        grown = mass * (1.0 - 0.1 * trait_ref[2, k]) + gain
        high, low = split2(grown)
        high = high.astype(BF16)
        return jnp.concatenate([high, low.astype(BF16), high], axis=0), above + leaf

    def body(i, above):
        k = bins - 1 - 2 * i
        first, above = one(k, above)
        second, above = one(k - 1, above)
        right = jnp.concatenate([first, second], axis=1)
        moved = jnp.dot(left_ref[...], right, preferred_element_type=F32)
        for j in range(2):
            part = moved[:, j * LANES : (j + 1) * LANES]
            total = part[0:patches] * weights[0]
            for t in range(1, kinds):
                total = total + part[t * patches : (t + 1) * patches] * weights[t]
            out_ref[pl.ds(k - j, patches, stride=bins), :] = total
        return above

    lax.fori_loop(0, bins // 2, body, jnp.zeros((patches, LANES), F32), unroll=4)


def river_kernel(
    slots,
    here_ref,
    arrived_ref,
    target_ref,
    mate_ref,
    water_ref,
    rate_ref,
    out_ref,
    hill_out_ref,
    room_ref,
    lo_refs,
    mask_refs,
    speed_refs,
    state_ref,
    value_ref,
    rows_left_ref,
    rows_lo_ref,
    hill_ref,
    hill_rate_ref,
    runoff_ref,
):
    chunks = state_ref.shape[1]
    rows = target_ref.shape[0]
    size = 2 * chunks + rows + 2
    peers = arrived_ref.shape[0] // size
    spans = 2 * chunks
    window = NSUB + 2
    base = here_ref[0]
    core = here_ref[1]
    other = 1 - core

    def block_of(b):
        j = base + b
        return jnp.where(j >= peers, j - peers, j)

    square = (LANES, LANES)
    lane = lane_iota(square).astype(F32)
    eye = jnp.where(row_iota(square) == lane_iota(square), 1.0, 0.0).astype(BF16)
    ones = jnp.ones(square, BF16)

    def table(pair, at, first=0, last=chunks):
        j = block_of(2 * pair + at)
        target = arrived_ref[pl.ds(j * size, chunks), :].astype(jnp.int32)
        span = target >> 7
        low = (target & 127).astype(F32)
        for h in range(first, last):
            if pair == 0:
                diagonal = jnp.broadcast_to(low[h : h + 1, :], square).astype(BF16) * eye
                column = jnp.dot(diagonal, ones, preferred_element_type=F32)
            else:
                column = jnp.broadcast_to(low[h : h + 1, :], square).T
            mask_refs[pair][at, h] = jnp.where(
                row_iota((spans, LANES)) == span[h : h + 1, :], 1.0, 0.0
            ).astype(BF16)
            lo_refs[pair][at, h * LANES : (h + 1) * LANES, :] = jnp.where(
                column == lane, 1.0, 0.0
            ).astype(BF16)
        if first == 0:
            speed_refs[pair][at] = arrived_ref[pl.ds(j * size + chunks, chunks), :]

    table(0, 0)
    table(0, 1)

    fraction = 1.0 / NSUB
    half = 3 * chunks
    for which in range(2):
        if which == 0:
            target = target_ref[...]
        else:
            target = mate_ref[3 * chunks :, :].astype(jnp.int32)
        span = target >> 7
        low = target & 127
        values = [split2(from_peers(arrived_ref, rows, slots, f, size - 2 + which, size)) for f in range(3)]
        for a in range(rows):
            mask = row_iota((chunks, LANES)) == span[a : a + 1, :]
            for s in range(2):
                for f in range(3):
                    m = (s * 3 + f) * chunks
                    rows_left_ref[which, a, m : m + chunks, :] = jnp.where(
                        mask, values[f][s][a : a + 1, :], 0.0
                    ).astype(BF16)
            rows_lo_ref[which, a] = jnp.where(
                row_iota((LANES, LANES)) == low[a : a + 1, :], 1.0, 0.0
            ).astype(BF16)
        taken = nt_dot(
            jnp.concatenate([rows_left_ref[which, a] for a in range(rows)], axis=1),
            jnp.concatenate([rows_lo_ref[which, a] for a in range(rows)], axis=1),
        )
        for f in range(3):
            runoff_ref[which, f] = fraction * (
                taken[f * chunks : (f + 1) * chunks]
                + taken[half + f * chunks : half + (f + 1) * chunks]
            )

    state_ref[...] = jnp.zeros_like(state_ref)
    for q in range(2):
        hill_ref[q] = unrow(water_ref[q : q + 1, :], chunks)
        hill_rate_ref[q] = unrow(rate_ref[q : q + 1, :], chunks)
    own = jnp.where(core == 0, water_ref[2:3, :], water_ref[3:4, :])
    state_ref[core] = unrow(own, chunks)
    state_ref[other] = mate_ref[0:chunks, :]
    hill_ref[2] = mate_ref[chunks : 2 * chunks, :]
    hill_rate_ref[2] = mate_ref[2 * chunks : 3 * chunks, :]
    deep = [jnp.where(core == 0, runoff_ref[which, 2], 0.0) for which in range(2)]
    surface = [runoff_ref[0, 0], runoff_ref[0, 1], runoff_ref[1, core]]

    def pair_flow(pair):
        outs = []
        for i in range(2):
            out = speed_refs[pair][i] * state_ref[2 * pair + i]
            high, low = split2(out)
            value_ref[pair, 2 * i] = high
            value_ref[pair, 2 * i + 1] = low
            outs.append(out)
        pieces = []
        for h in range(chunks):
            masks = [mask_refs[pair][i, h] for i in range(2)]
            pieces.append(
                jnp.concatenate(
                    [
                        jnp.broadcast_to(value_ref[pair, m, h : h + 1, :], (spans, LANES)).astype(BF16)
                        * masks[m // 2]
                        for m in range(4)
                    ],
                    axis=0,
                )
            )
        flow = jnp.dot(
            jnp.concatenate(pieces, axis=1),
            jnp.concatenate([lo_refs[pair][0], lo_refs[pair][1]], axis=1),
            preferred_element_type=F32,
        )
        flows = []
        for i in range(2):
            part = flow[2 * i * spans : 2 * (i + 1) * spans, i * LANES : (i + 1) * LANES]
            flows.append(part[0:spans] + part[spans:])
        return outs, flows

    def advance(pairs, build=None, send=None):
        order = list(reversed(range(pairs)))
        for place, pair in enumerate(order):
            if build is not None:
                build(chunks * place // pairs, chunks * (place + 1) // pairs)
            outs, flows = pair_flow(pair)
            b = 2 * pair
            if send is not None and pair + 2 < pairs + 1:
                send(b + 4)
                send(b + 5)
            state_ref[b + 2] += flows[1][chunks:]
            state_ref[b + 1] = state_ref[b + 1] - outs[1] + flows[1][:chunks] + flows[0][chunks:]
            state_ref[b] = state_ref[b] - outs[0] + flows[0][:chunks]
        gone = [hill_rate_ref[i] * hill_ref[i] for i in range(3)]
        for i in range(3):
            hill_ref[i] = hill_ref[i] - gone[i] + surface[i]
        state_ref[core] += jnp.where(core == 0, gone[0], gone[1]) + deep[0]
        state_ref[other] += gone[2] + deep[1]

    shape = (peers, LANES)
    section = lane_iota(shape) // slots
    extra = -(-window * slots // LANES)
    out_size = chunks + extra
    reached = [jnp.zeros(shape, F32) for _ in range(extra)]

    def send(b):
        if b >= window:
            return
        j = block_of(b)
        state = state_ref[b]
        out_ref[pl.ds(j * out_size, chunks), :] = state
        index = arrived_ref[pl.ds(j * size + spans, rows), :].astype(jnp.int32)
        value = by_peer(look_up(state, index), peers, slots)
        e, at = divmod(b * slots, LANES)
        reached[e] = jnp.where(section == at // slots, value, reached[e])

    table(1, 0)
    table(1, 1)
    advance(1)
    for pairs in range(2, NSUB // 2 + 1):

        for i in range(2):
            advance(pairs, build=functools.partial(table, pairs, i))
    advance(NSUB // 2 + 1, send=send)
    for b in range(4):
        send(b)

    hill_out_ref[...] = hill_ref[0:2]

    room = arrived_ref[pl.ds(size - 2, peers, stride=size), :]
    room_ref[...] = all_sections(jnp.where(section == 3, room, 0.0), slots)
    for e in range(extra):
        out_ref[pl.ds(chunks + e, peers, stride=out_size), :] = reached[e]


def survive_kernel(
    bins,
    slots,
    window,
    here_ref,
    trait_ref,
    part_ref,
    hill_ref,
    room_ref,
    share_ref,
    source_ref,
    moved_ref,
    out_ref,
    flooded_ref,
    state_ref,
    alive_ref,
    wet_ref,
):
    peers = room_ref.shape[0]
    chunks = hill_ref.shape[1]
    size = part_ref.shape[0] // peers

    @pl.when(pl.program_id(0) == 0)
    def _():
        channel = [jnp.zeros((chunks, LANES), F32)] * 2
        for b in range(0, window, 2):
            j = here_ref[0] - b
            j = jnp.where(j < 0, j + peers, j)
            for q in range(2):
                channel[q] = channel[q] + part_ref[pl.ds((j + q) * size, chunks), :]
        for q in range(2):
            for h in range(chunks):
                at = slice(h * LANES, (h + 1) * LANES)
                state_ref[q : q + 1, at] = hill_ref[q, h : h + 1, :]
                state_ref[2 + q : 3 + q, at] = channel[q][h : h + 1, :]

        shape = (peers, LANES)
        section = lane_iota(shape) // slots
        even = row_iota(shape) % 2 == 0
        stored = jnp.zeros(shape, F32)
        for e in range(size - chunks):
            part = part_ref[pl.ds(chunks + e, peers, stride=size), :]
            part = part + jnp.where(even, pltpu.roll(part, peers - 1, 0), pltpu.roll(part, 1, 0))
            for b in range(window):
                if b * slots // LANES != e:
                    continue
                moved = pltpu.roll(part, b, 0) if b else part
                mine = (section == b * slots % LANES // slots) & (even == (b % 2 == 0))
                stored = stored + jnp.where(mine, moved, 0.0)
        stored = all_sections(stored, slots)
        wet_ref[...] = stored / (stored + room_ref[...])

        rows = share_ref.shape[0]
        value = share_ref[...] * from_peers(wet_ref, rows, slots)
        source = source_ref[...]
        total = jnp.zeros((LANES, LANES), F32)
        for a in range(rows):
            total = total + jnp.where(
                row_iota((LANES, LANES)) == source[a : a + 1, :], value[a : a + 1, :], 0.0
            )
        flooded = jnp.sum(total.T, axis=0, keepdims=True)
        flooded_ref[...] = flooded
        for k in range(bins):
            alive_ref[k : k + 1, :] = jnp.exp(-trait_ref[3, k] * flooded)

    alive = alive_ref[...]
    base = pl.program_id(0) * out_ref.shape[0]
    for p in range(out_ref.shape[0] // bins):
        at = pl.ds(pl.multiple_of(base + p * bins, bins), bins)
        out_ref[p * bins : (p + 1) * bins, :] = moved_ref[at, :] * alive


def shards(
    axes,
    biomass,
    patch_area,
    cohort_traits,
    cell_forcing,
    disturb_weight,
    transitions,
    land_source,
    pair_share,
    river_target,
    downstream_step,
    river_water,
    river_rates,
    capacity,
):
    patches, bins, lands = biomass.shape
    rivers = river_water.shape[1]
    peers = math.prod(lax.axis_size(a) for a in axes)
    slots = land_source.shape[0] // peers
    rows = land_source.shape[0] // LANES
    chunks = rivers // LANES
    kinds = transitions.shape[0]
    window = NSUB + 2
    place = lax.axis_index(axes).astype(jnp.int32)
    here = jnp.stack([place - place % 2, place % 2])

    bio = biomass.reshape(patches * bins, lands)
    source = land_source.reshape(rows, LANES)
    share = pair_share.reshape(rows, LANES)
    target = river_target.reshape(rows, LANES)
    step = downstream_step.reshape(chunks, LANES)

    def exchange(message, size):
        inner = math.gcd(size, 8)
        message = message.reshape(peers, size // inner, inner, LANES)
        arrived = lax.all_to_all(message, axes, split_axis=0, concat_axis=0, tiled=True)
        return on_chip(arrived.reshape(peers * size, LANES))

    size = 2 * chunks + rows + 2
    tile = patches // 2
    whole = lambda *shape: pl.BlockSpec(shape, lambda i: (0,) * len(shape))
    message, mate = pl.pallas_call(
        functools.partial(rain_kernel, bins, slots),
        grid=(patches // tile,),
        out_shape=(
            pltpu.VMEM((peers * size, LANES), F32),
            pltpu.VMEM((3 * chunks + rows, LANES), F32),
        ),
        in_specs=[
            SMEM,
            SMEM,
            pl.BlockSpec((tile * bins, LANES), lambda i: (i, 0)),
            pl.BlockSpec((tile, LANES), lambda i: (i, 0)),
            whole(5, LANES),
            whole(rows, LANES),
            whole(rows, LANES),
            whole(chunks, LANES),
            whole(rows, LANES),
            whole(4, rivers),
            whole(4, rivers),
            whole(chunks, LANES),
        ],
        out_specs=(whole(peers * size, LANES), whole(3 * chunks + rows, LANES)),
        scratch_shapes=[pltpu.VMEM((1, LANES), F32), pltpu.VMEM((2, bins, LANES), F32)],
        name="rain",
    )(
        here[1:2],
        cohort_traits,
        bio,
        patch_area,
        cell_forcing,
        source,
        share,
        step,
        target,
        river_water,
        river_rates,
        capacity.reshape(chunks, LANES),
    )
    arrived = exchange(message, size)
    mate = on_chip(lax.ppermute(mate, axes, [(i, i + 1 - 2 * (i % 2)) for i in range(peers)]))

    moved = pl.pallas_call(
        functools.partial(transit_kernel, kinds, bins),
        out_shape=pltpu.VMEM((patches * bins, LANES), F32),
        in_specs=[SMEM, VMEM, VMEM, VMEM, VMEM],
        out_specs=VMEM,
        scratch_shapes=[pltpu.VMEM((kinds * patches, 3 * patches), BF16)],
        name="transit",
    )(cohort_traits, transitions.reshape(kinds * patches, patches), bio, cell_forcing, disturb_weight)

    spans = 2 * chunks
    out_size = chunks - (-window * slots // LANES)
    parts, hill, room = pl.pallas_call(
        functools.partial(river_kernel, slots),
        out_shape=(
            pltpu.VMEM((peers * out_size, LANES), F32),
            pltpu.VMEM((2, chunks, LANES), F32),
            pltpu.VMEM((peers, LANES), F32),
        ),
        in_specs=[SMEM] + [VMEM] * 5,
        out_specs=(VMEM, VMEM, VMEM),
        scratch_shapes=[
            [pltpu.VMEM((2, rivers, LANES), BF16)] * (window // 2),
            [pltpu.VMEM((2, chunks, spans, LANES), BF16)] * (window // 2),
            [pltpu.VMEM((2, chunks, LANES), F32)] * (window // 2),
            pltpu.VMEM((window + 1, chunks, LANES), F32),
            pltpu.VMEM((window // 2, 4, chunks, LANES), F32),
            pltpu.VMEM((2, rows, 6 * chunks, LANES), BF16),
            pltpu.VMEM((2, rows, LANES, LANES), BF16),
            pltpu.VMEM((3, chunks, LANES), F32),
            pltpu.VMEM((3, chunks, LANES), F32),
            pltpu.VMEM((2, 3, chunks, LANES), F32),
        ],
        compiler_params=pltpu.CompilerParams(vmem_limit_bytes=48 << 20),
        name="river",
    )(here, arrived, target, mate, river_water, river_rates)
    parts = exchange(parts, out_size)

    tile = patches // 2
    new_biomass, flooded, river_state = pl.pallas_call(
        functools.partial(survive_kernel, bins, slots, window),
        grid=(patches // tile,),
        out_shape=(
            jax.ShapeDtypeStruct((patches * bins, LANES), F32),
            jax.ShapeDtypeStruct((1, LANES), F32),
            jax.ShapeDtypeStruct((4, rivers), F32),
        ),
        in_specs=[
            SMEM,
            SMEM,
            VMEM,
            VMEM,
            VMEM,
            whole(rows, LANES),
            whole(rows, LANES),
            VMEM,
        ],
        out_specs=(
            pl.BlockSpec((tile * bins, LANES), lambda i: (i, 0)),
            whole(1, LANES),
            whole(4, rivers),
        ),
        scratch_shapes=[pltpu.VMEM((bins, LANES), F32), pltpu.VMEM((peers, LANES), F32)],
        name="survive",
    )(here, cohort_traits, parts, on_chip(hill), on_chip(room), share, source, on_chip(moved))
    return (new_biomass.reshape(patches, bins, lands), flooded.reshape(lands), river_state)


def solution(mesh):
    axes = tuple(mesh.axis_names)
    split = P(axes)
    split1 = P(None, axes)

    def body(*args):
        return shards(axes, *args)

    return jax.shard_map(
        body,
        mesh=mesh,
        in_specs=(
            P(None, None, axes),
            split1,
            P(),
            split1,
            split1,
            P(),
            split,
            split,
            split,
            split,
            split1,
            split1,
            split,
        ),
        out_specs=(P(None, None, axes), split, split1),
        check_vma=False,
    )
```
